256 devices in a mesh: dp: 32 (over x, z), head: 8 (over y, core).
Axes of the slice: x: 4, y: 4, z: 8, core: 2. Of those that a mesh axis runs over, the one named last changes fastest.
Arguments:
- tokens: bfloat16 [16384, 4096], P('dp'), may hold values from -6 to 6
- q_weight: bfloat16 [4096, 8192], P('dp', 'head'), may hold values from -0.09375 to 0.09375
- kv_weight: bfloat16 [4096, 1024], P('dp', 'head'), may hold values from -0.09375 to 0.09375
- q_gain: float32 [128], replicated, may hold values from 0.1 to 1.9
- k_gain: float32 [128], replicated, may hold values from 0.1 to 1.9
- doc_lengths: int32 [32, 16], replicated, may hold values from 0 to 512, as said below
Outputs:
- attended: bfloat16 [16384, 8192], P('dp', 'head')
The draws below stay inside these ranges and needn't reach their ends.
Inputs may be any that keep to these rules, and one draw needn't show every extreme that they name: `doc_lengths`: row r lists the lengths of the documents packed in order on index r of dp and sums to 512; some rank holds a single document of 512 tokens.
All inputs are finite; a program needn't handle non-finite values.
Results may differ from the reference program's by a relative error of at most 0.0068.
Values may be sent and summed in bfloat16 or wider, within the bound.
A program may use at most 64 MiB of HBM per device.

```python
import math
import jax
import jax.numpy as jnp
from jax import lax

D = 4096
QH = 64
KVH = 4
HD = 128
TOK_DEV = 512
NDOC = 16
TOKENS = 16384
N_DP = 32


def draw_doc_lengths(key, part):
    key_count, key_weight, key_rank = jax.random.split(jax.random.fold_in(key, 7), 3)
    rank_ids = jnp.arange(N_DP, dtype=jnp.int32)
    doc_count = jax.random.randint(key_count, (N_DP, 1), 1, NDOC + 1)
    single_rank = jax.random.randint(key_rank, (), 0, N_DP)
    doc_count = jnp.where(rank_ids[:, None] == single_rank, 1, doc_count)
    weights = jax.random.randint(key_weight, (N_DP, NDOC), 1, 9)
    weights = jnp.where(jnp.arange(NDOC, dtype=jnp.int32)[None, :] < doc_count, weights, 0)
    weight_sum = jnp.sum(weights, axis=1, keepdims=True)
    lengths = weights * TOK_DEV // weight_sum
    shortfall = TOK_DEV - jnp.sum(lengths, axis=1, keepdims=True)
    lengths = jnp.where(jnp.arange(NDOC, dtype=jnp.int32)[None, :] == 0, lengths + shortfall, lengths)
    return lengths.astype(jnp.int32)


def block_scale(stream_key, extent, cuts, low, high):
    def one(dim, shards_of):
        draws = jax.random.uniform(jax.random.fold_in(jax.random.fold_in(stream_key, 6), dim), (shards_of,), jnp.float32, low / len(cuts), high / len(cuts))
        return jnp.repeat(jnp.exp(draws), extent[dim] // shards_of).reshape((-1,) + (1,) * (len(extent) - dim - 1))

    loudness = one(*cuts[0])
    for cut in cuts[1:]:
        loudness = loudness * one(*cut)
    return loudness


def normal_values(stream_key, shape, scale, reach, shards=(), held_as=jnp.bfloat16):
    loudness = block_scale(stream_key, shape, shards, -0.22, 0.18) if shards else 1.0
    drawn = jax.random.normal(stream_key, shape, jnp.float32) * scale * loudness
    return jnp.minimum(jnp.maximum(drawn, -reach), reach).astype(held_as)


def setup_inputs(seed: int = 0) -> dict:
    splits = jax.random.split(jax.random.key(seed), 7)
    return {
        "tokens": normal_values(splits[0], (TOKENS, D), 1.0, 6.0, ((0, 32),)),
        "q_weight": normal_values(splits[1], (D, QH * HD), D ** -0.5, 0.09375, ((0, 32), (1, 8))),
        "kv_weight": normal_values(splits[2], (D, 2 * KVH * HD), D ** -0.5, 0.09375, ((0, 32), (1, 8))),
        "q_gain": jnp.clip(1.0 + 0.18 * jax.random.normal(splits[3], (HD,), jnp.float32), 0.1, 1.9),
        "k_gain": jnp.clip(1.0 + 0.18 * jax.random.normal(splits[4], (HD,), jnp.float32), 0.1, 1.9),
        "doc_lengths": draw_doc_lengths(jax.random.fold_in(splits[6], 71), 0),
    }


theta_base = 1000000.0
norm_eps = 1e-06

def doc_layout(lengths, count):
    doc_ends = jnp.cumsum(lengths).astype(jnp.int32)
    places = jnp.arange(count, dtype=jnp.int32)
    passed = (places[:, None] >= doc_ends[None, :]).astype(jnp.int32)
    doc_ids = lax.optimization_barrier(jnp.sum(passed, axis=1)).astype(jnp.int32)
    starts = lax.optimization_barrier(jnp.sum(passed * lengths[None, :], axis=1)).astype(jnp.int32)
    return (doc_ids, places - starts)

def norm_rope(raw, gain, positions):
    half_width = raw.shape[-1] // 2
    inv_rms = lax.rsqrt(lax.optimization_barrier(jnp.mean(raw * raw, axis=-1, keepdims=True)) + norm_eps)
    normed = raw * inv_rms * gain
    frequency = jnp.exp(jnp.arange(half_width, dtype=jnp.float32) * (-2.0 * math.log(theta_base) / raw.shape[-1]))
    angles = positions.astype(jnp.float32)[:, None] * frequency[None, :]
    cosine = jnp.cos(angles)[:, None, :]
    sine_table = jnp.sin(angles)[:, None, :]
    lower_half = normed[..., :half_width]
    second = normed[..., half_width:]
    return jnp.concatenate([lower_half * cosine - second * sine_table, second * cosine + lower_half * sine_table], axis=-1).astype(jnp.bfloat16)

def reference(tokens, q_weight, kv_weight, q_gain, k_gain, doc_lengths):
    head_group = QH // KVH

    def one_rank(rank_index):
        token_rows = lax.dynamic_slice_in_dim(tokens, rank_index * TOK_DEV, TOK_DEV, 0)
        lengths = lax.dynamic_index_in_dim(doc_lengths, rank_index, 0, keepdims=False)
        doc_ids, positions = doc_layout(lengths, TOK_DEV)
        places = jnp.arange(TOK_DEV, dtype=jnp.int32)
        q_raw = jnp.dot(token_rows, q_weight, preferred_element_type=jnp.float32).reshape(TOK_DEV, QH, HD)
        kv_raw = jnp.dot(token_rows, kv_weight, preferred_element_type=jnp.float32)
        k_raw = kv_raw[:, :KVH * HD].reshape(TOK_DEV, KVH, HD)
        values = kv_raw[:, KVH * HD:].reshape(TOK_DEV, KVH, HD).astype(jnp.bfloat16)
        queries = norm_rope(q_raw, q_gain, positions).reshape(TOK_DEV, KVH, head_group, HD)
        key_rows = norm_rope(k_raw, k_gain, positions)
        scores = jnp.einsum('qkgd,tkd->kgqt', queries.astype(jnp.float32), key_rows.astype(jnp.float32)) * HD ** (-0.5)
        allowed = (doc_ids[:, None] == doc_ids[None, :]) & (places[:, None] >= places[None, :])
        weights = jnp.where(allowed[None, None], jnp.exp(scores), 0.0)
        weights_bf = (weights / lax.optimization_barrier(jnp.sum(weights, axis=-1, keepdims=True))).astype(jnp.bfloat16)
        mixed_out = jnp.einsum('kgqt,tkd->qkgd', weights_bf.astype(jnp.float32), values.astype(jnp.float32))
        return mixed_out.astype(jnp.bfloat16).reshape(TOK_DEV, QH * HD)
    stacked = lax.map(one_rank, jnp.arange(N_DP, dtype=jnp.int32))
    return stacked.reshape(TOK_DEV * N_DP, QH * HD)
```

```python
import functools
import math

import jax
import jax.numpy as jnp
import numpy as np
from jax import lax
from jax.experimental import pallas as pl
from jax.experimental.pallas import tpu as pltpu
from jax.sharding import PartitionSpec as P

HD = 128
ROWS = 512
FEAT = 4096
THETA = 1000000.0
EPS = 1e-06
MESH = pl.DeviceIdType.MESH
F32 = jnp.float32
BF16 = jnp.bfloat16
N_SEND = 224
GROUPS = (0, 1, 2)
OWN, NEAR, PAIR, FAR = 0, 1, 2, 3


def kernel(tok, w, kvw, qg, kg, freq, dl, out,
           tokb, wbuf, kvbuf, acc, kvacc, kvst, kvin, cosb, sinb, bias, ost,
           send, rw, rt, rs, rkv, rout, loc):
    dp = lax.axis_index("dp")
    hd = lax.axis_index("head")
    x, z = dp // 8, dp % 8
    y, c = hd // 2, hd % 2
    side = x // 2
    xn, xp = x + 1 - 2 * (x % 2), 3 - x
    worker = c == side
    is_v = y // 2
    kv_to = 2 * (y % 2) + side

    def dev(xx, zz, yy, cc):
        return (xx * 8 + zz, yy * 2 + cc)

    near = dev(xn, z, y, c)
    pair = dev(xp, z, y, c)
    up, down = dev(x, (z + 1) % 8, y, c), dev(x, (z + 7) % 8, y, c)
    yup, ydown = dev(x, z, (y + 1) % 4, c), dev(x, z, (y + 3) % 4, c)
    sib = dev(x, z, y, 1 - c)

    barrier = pltpu.get_barrier_semaphore()
    for peer in (near, pair, up, down, yup, ydown, sib):
        pl.semaphore_signal(barrier, inc=1, device_id=peer, device_id_type=MESH)
    src_side = y % 2
    src_x = jnp.where(side == src_side, x, xp)
    kv_self = worker & (kv_to == y)
    for v in (0, 1):
        src_y = 2 * v + y // 2
        @pl.when(jnp.logical_not(kv_self & (is_v == v)))
        def _():
            pl.semaphore_signal(
                barrier, inc=1, device_id=dev(src_x, z, src_y, src_side), device_id_type=MESH)
    extra = jnp.where(worker, jnp.where(kv_to == y, 3, 4), 0)
    pl.semaphore_wait(barrier, 7 + extra)

    used = [0]
    pending = {"all": [], "worker": [], "helper": [], "beyond": []}

    def push(src, dst, rsem, to, who="all"):
        n = used[0]
        used[0] += 1
        pending[who].append((n, dst))
        pltpu.make_async_remote_copy(
            src_ref=src(), dst_ref=dst(), send_sem=send.at[n], recv_sem=rsem,
            device_id=to, device_id_type=MESH).start()

    def drain(who):
        for n, dst in pending[who]:
            arrive(dst(), send.at[n])

    def arrive(dst, rsem):
        pltpu.make_async_copy(dst, dst, rsem).wait()

    def slot(g, q, xi):
        at, lo, n = (q, 0, 128) if q < 7 else (7, 64 * (q - 7), 64)
        buf = kvbuf if g == 0 else wbuf.at[g - 1]
        return buf.at[at, pl.ds(xi * 128 + lo, n), :]

    def half(g, q, xi, h):
        buf = kvbuf if g == 0 else wbuf.at[g - 1]
        return buf.at[q, pl.ds(xi * 128 + 64 * h, 64), :]

    def source(g, of_side):
        if g == 0:
            return kvw
        return w.at[:, pl.ds(pl.multiple_of(of_side * 512 + (g - 1) * 256, 256), 256)]

    def guarded(g, fn):
        if g == 0:
            pl.when(worker)(fn)
        else:
            fn()

    def who(g):
        return "worker" if g == 0 else "all"

    def wait_w(g, q, xi):
        arrive(slot(g, q, xi), rw.at[g, q, xi])

    def ring_first(g, xi, src):
        push(src, lambda: slot(g, 1, xi), rw.at[g, 1, xi], up, who(g))
        push(src, lambda: slot(g, 2, xi), rw.at[g, 2, xi], down, who(g))

    def cross(g, q):
        push(lambda: slot(g, q, PAIR), lambda: slot(g, q, FAR), rw.at[g, q, FAR], near, who(g))

    def start_pair(g):
        if g == 0:
            @pl.when(jnp.logical_not(worker))
            def _():
                push(lambda: kvw, lambda: slot(0, 0, PAIR), rw.at[0, 0, PAIR], pair, "helper")
        else:
            push(lambda: source(g, 1 - side), lambda: slot(g, 0, PAIR), rw.at[g, 0, PAIR], pair)

    def start_near(g):
        guarded(g, lambda: push(lambda: source(g, side), lambda: slot(g, 0, NEAR), rw.at[g, 0, NEAR], near, who(g)))

    def start_own(g):
        guarded(g, lambda: ring_first(g, OWN, lambda: source(g, side)))

    def begin_near(g):
        def go():
            wait_w(g, 0, NEAR)
            ring_first(g, NEAR, lambda: slot(g, 0, NEAR))
        guarded(g, go)

    def begin_pair(g):
        def go():
            wait_w(g, 0, PAIR)
            ring_first(g, PAIR, lambda: slot(g, 0, PAIR))
            cross(g, 0)
        guarded(g, go)

    def ring(g, k, items=(PAIR, OWN, NEAR)):
        def go():
            for xi in items:
                for d in (0, 1):
                    q = 2 * k - 1 + d
                    wait_w(g, q, xi)
                    to = (up, down)[d]
                    if k < 3:
                        push(lambda: slot(g, q, xi), lambda q=q, xi=xi: slot(g, q + 2, xi), rw.at[g, q + 2, xi], to, who(g))
                    elif k == 3:
                        push(lambda: half(g, q, xi, d), lambda d=d, xi=xi: slot(g, 7 + d, xi), rw.at[g, 7 + d, xi], to, who(g))
                    if xi == PAIR:
                        cross(g, q)
        guarded(g, go)

    def far(g, qs):
        def go():
            for q in qs:
                wait_w(g, q, FAR)
        guarded(g, go)

    def cols(head_of):
        return pl.ds(pl.multiple_of(head_of * 512, 512), 512)

    def piece(j, head_of):
        return tokb.at[1, pl.ds(128 * j, 128), cols(head_of)]

    y_of = ((y) % 4, (y + 3) % 4, (y + 1) % 4, (y + 2) % 4)

    def tok_mine(j):
        ref = lambda: piece(j, hd)
        arrive(ref(), rt.at[0, j])
        push(ref, ref, rt.at[1, j], yup)
        push(ref, ref, rt.at[2, j], ydown)
        push(ref, ref, rs.at[0, j], sib)

    def tok_side(src, j):
        ref = lambda: piece(j, y_of[src] * 2 + c)
        arrive(ref(), rt.at[src, j])
        if src == 1 and j < 2:
            push(ref, ref, rt.at[3, j], yup)
        if src == 2 and j >= 2:
            push(ref, ref, rt.at[3, j], ydown)
        push(ref, ref, rs.at[src, j], sib)

    def tok_sib():
        for src in range(4):
            for j in range(4):
                arrive(piece(j, y_of[src] * 2 + 1 - c), rs.at[src, j])

    start_pair(0)
    start_pair(1)
    start_near(0)
    start_own(0)
    start_near(1)
    start_own(1)
    for j in (0, 1):
        push(lambda: tok.at[pl.ds(128 * j, 128), cols(hd)], lambda j=j: piece(j, hd), rt.at[0, j], pair)
    start_pair(2)
    for j in (2, 3):
        push(lambda: tok.at[pl.ds(128 * j, 128), cols(hd)], lambda j=j: piece(j, hd), rt.at[0, j], pair)
    start_near(2)

    load_tok = pltpu.make_async_copy(tok, tokb.at[0], loc.at[0])
    load_tok.start()
    load_w = []
    for g in (1, 2):
        load_w.append(pltpu.make_async_copy(source(g, side), slot(g, 0, OWN), loc.at[g]))
        load_w[-1].start()
    load_kv = pltpu.make_async_copy(kvw, slot(0, 0, OWN), loc.at[3])
    load_kv.start()

    def tables(t):
        rank = dp if t == 0 else xp * 8 + z
        row = lax.broadcasted_iota(jnp.int32, (ROWS, HD), 0)
        lane = lax.broadcasted_iota(jnp.int32, (ROWS, HD), 1)
        start = jnp.zeros((ROWS, HD), jnp.int32)
        end = 0
        for d in range(16):
            n = dl[rank, d]
            end = end + n
            start = start + jnp.where(row >= end, n, 0)
        angle = (row - start).astype(F32) * freq[...]
        cosb[t] = jnp.cos(angle)
        s = jnp.sin(angle)
        sinb[t] = jnp.where(lane < 64, -s, s)
        for j in range(4):
            col = lane + 128 * j
            bias[t, :, 128 * j:128 * j + 128] = jnp.where(
                (col >= start) & (col <= row), 0.0, -1e30)

    def norm_rope(u, gain, t):
        ms = jnp.mean(u * u, axis=-1, keepdims=True)
        n = u * lax.rsqrt(ms + EPS) * gain
        return (n * cosb[t] + pltpu.roll(n, 64, 1) * sinb[t]).astype(BF16)

    def lhs(t, p):
        k = (p + 1) // 2
        zz = (z + 8 + k - 2 * k * (p % 2)) % 8
        parts = []
        for xx in (x, xn, xp, 3 - xn):
            f = pl.multiple_of((xx * 8 + zz) * 128, 128)
            parts.append(tokb[t, :, pl.ds(f, 128)])
        return jnp.concatenate(parts, axis=1)

    def dots(t, ps, gs=(1, 2)):
        def body(p, _):
            a = lhs(t, p)
            for g in gs:
                acc[t, g - 1] += jnp.dot(a, wbuf[g - 1, p], preferred_element_type=F32)
            return 0
        lax.fori_loop(ps[0], ps[1], body, 0)

    def kv_product(t):
        @pl.when(worker)
        def _():
            kvacc[...] = jnp.zeros_like(kvacc)

            def body(p, _):
                kvacc[...] += jnp.dot(lhs(t, p), kvbuf[p], preferred_element_type=F32)
                return 0
            lax.fori_loop(0, 8, body, 0)

            @pl.when(is_v == 0)
            def _():
                kvst[t] = norm_rope(kvacc[...], kg[...], t)

            @pl.when(is_v == 1)
            def _():
                kvst[t] = kvacc[...].astype(BF16)

    def kv_send(t):
        @pl.when(worker)
        def _():
            for xx, tt in ((x, t), (xp, 1 - t)):
                def send_to(core, kind):
                    push(lambda: kvst.at[t], lambda tt=tt: kvin.at[is_v, tt],
                         rkv.at[is_v, tt], dev(xx, z, kv_to, core), kind)
                send_to(1 - c, "worker")
                if tt != t:
                    send_to(c, "worker")
                    continue
                pl.when(kv_to != y)(lambda: send_to(c, "beyond"))

                @pl.when(kv_to == y)
                def _():
                    pltpu.make_async_copy(kvst.at[t], kvin.at[is_v, t], rkv.at[is_v, t]).start()

    scale = HD ** -0.5 * math.log2(math.e)

    def attend(t, g, hh):
        q = norm_rope(acc[t, g - 1, :, 128 * hh:128 * hh + 128], qg[...], t)
        for i in (0, 1):
            m = 256 * (i + 1)
            s = lax.dot_general(q[256 * i:m], kvin[0, t, :m], (((1,), (1,)), ((), ())),
                                preferred_element_type=F32)
            e = jnp.exp2(s * scale + bias[t, 256 * i:m, :m])
            probs = (e * (1.0 / jnp.sum(e, axis=-1, keepdims=True))).astype(BF16)
            o = jnp.dot(probs, kvin[1, t, :m], preferred_element_type=F32)
            ost[t, 256 * i:m, (g - 1) * 256 + 128 * hh:(g - 1) * 256 + 128 * hh + 128] = o.astype(BF16)

    def emit(t, g):
        here = ost.at[t, :, pl.ds(256 * (g - 1), 256)]
        there = out.at[:, pl.ds(pl.multiple_of(side * 512 + 256 * (g - 1), 256), 256)]
        if t == 1:
            push(lambda: here, lambda: there, rout.at[g - 1], pair)
        else:
            pltpu.make_async_copy(here, there, loc.at[3 + g]).start()

    acc[...] = jnp.zeros_like(acc)
    begin_near(0)
    begin_pair(0)
    begin_near(1)
    begin_pair(1)
    tables(0)
    ring(0, 1)
    start_own(2)
    tok_mine(0)
    ring(0, 2)
    begin_near(2)
    tok_mine(1)
    tables(1)
    ring(0, 3)
    begin_pair(2)
    tok_mine(2)
    ring(1, 1)
    ring(0, 4)
    tok_mine(3)
    for j in (0, 1):
        tok_side(1, j)
        tok_side(2, j)
    load_tok.wait()
    load_kv.wait()
    for cp in load_w:
        cp.wait()
    far(0, range(9))
    kv_product(0)
    kv_send(0)
    ring(2, 1)
    for j in (2, 3):
        tok_side(1, j)
        tok_side(2, j)
    far(1, (0,))
    far(2, (0,))
    dots(0, (0, 1))
    ring(1, 2)
    for j in range(4):
        tok_side(3, j)
    far(1, (1, 2))
    far(2, (1, 2))
    dots(0, (1, 3))
    ring(2, 2)
    tok_sib()
    kv_product(1)
    kv_send(1)
    far(1, (3, 4))
    far(2, (3, 4))
    dots(0, (3, 5))
    dots(1, (0, 5))
    ring(1, 3)
    ring(2, 3)
    ring(1, 4, (PAIR,))
    ring(2, 4, (PAIR,))
    far(1, (5, 6))
    far(2, (5, 6))
    dots(0, (5, 7))
    dots(1, (5, 7))
    ring(1, 4, (OWN, NEAR))
    far(1, (7, 8))
    dots(1, (7, 8), (1,))
    dots(0, (7, 8), (1,))
    for v in (0, 1):
        for t in (1, 0):
            arrive(kvin.at[v, t], rkv.at[v, t])
    for hh in (0, 1):
        attend(1, 1, hh)
    for hh in (0, 1):
        attend(0, 1, hh)
    emit(1, 1)
    emit(0, 1)
    ring(2, 4, (OWN, NEAR))
    far(2, (7, 8))
    dots(1, (7, 8), (2,))
    for hh in (0, 1):
        attend(1, 2, hh)
    dots(0, (7, 8), (2,))
    emit(1, 2)
    for hh in (0, 1):
        attend(0, 2, hh)
    emit(0, 2)

    drain("all")
    pl.when(worker)(lambda: drain("worker"))
    pl.when(worker & (kv_to != y))(lambda: drain("beyond"))
    pl.when(jnp.logical_not(worker))(lambda: drain("helper"))
    for g in (1, 2):
        here = ost.at[0, :, pl.ds(256 * (g - 1), 256)]
        there = out.at[:, pl.ds(pl.multiple_of(side * 512 + 256 * (g - 1), 256), 256)]
        pltpu.make_async_copy(here, there, loc.at[3 + g]).wait()
        other = out.at[:, pl.ds(pl.multiple_of((1 - side) * 512 + 256 * (g - 1), 256), 256)]
        arrive(other, rout.at[g - 1])
    assert used[0] <= N_SEND, used[0]


def shards(tokens, q_weight, kv_weight, q_gain, k_gain, doc_lengths):
    half = np.exp(np.arange(64) * (-2.0 * math.log(THETA) / HD)).astype(np.float32)
    freq = jnp.asarray(np.concatenate([half, half])[None, :])
    vm = pl.BlockSpec(memory_space=pltpu.VMEM)
    any_ = pl.BlockSpec(memory_space=pl.ANY)
    dma = pltpu.SemaphoreType.DMA
    return pl.pallas_call(
        kernel,
        out_shape=jax.ShapeDtypeStruct((ROWS, 1024), BF16),
        in_specs=[any_, any_, any_, vm, vm, vm, pl.BlockSpec(memory_space=pltpu.SMEM)],
        out_specs=any_,
        scratch_shapes=[
            pltpu.VMEM((2, ROWS, FEAT), BF16),
            pltpu.VMEM((2, 8, 512, 256), BF16),
            pltpu.VMEM((8, 512, 128), BF16),
            pltpu.VMEM((2, 2, ROWS, 256), F32),
            pltpu.VMEM((ROWS, 128), F32),
            pltpu.VMEM((2, ROWS, 128), BF16),
            pltpu.VMEM((2, 2, ROWS, 128), BF16),
            pltpu.VMEM((2, ROWS, HD), F32),
            pltpu.VMEM((2, ROWS, HD), F32),
            pltpu.VMEM((2, ROWS, ROWS), F32),
            pltpu.VMEM((2, ROWS, 512), BF16),
            dma((N_SEND,)),
            dma((3, 9, 4)),
            dma((4, 4)),
            dma((4, 4)),
            dma((2, 2)),
            dma((2,)),
            dma((6,)),
        ],
        compiler_params=pltpu.CompilerParams(
            collective_id=0, has_side_effects=True, vmem_limit_bytes=60 * 2**20),
        cost_estimate=pl.CostEstimate(
            flops=6_000_000_000, bytes_accessed=12 * 2**20, transcendentals=2**21),
    )(tokens, q_weight, kv_weight, q_gain[None, :], k_gain[None, :], freq, doc_lengths)


def solution(mesh):
    placed = (P("dp", None), P("dp", "head"), P("dp", "head"), P(), P(), P())
    return jax.shard_map(
        shards, mesh=mesh, in_specs=placed, out_specs=P("dp", "head"), check_vma=False
    )
```

```python
import functools
import math

import jax
import jax.numpy as jnp
import numpy as np
from jax import lax
from jax.experimental import pallas as pl
from jax.experimental.pallas import tpu as pltpu
from jax.sharding import PartitionSpec as P

HD = 128
ROWS = 512
FEAT = 4096
THETA = 1000000.0
EPS = 1e-06
MESH = pl.DeviceIdType.MESH
F32 = jnp.float32
BF16 = jnp.bfloat16
S_KV, S_HELP, S_TOK, S_KEYS, S_BEYOND, S_OUT, S_SHARE = 0, 3, 4, 5, 6, 7, 8
GROUPS = (0, 1, 2)
OWN, NEAR, PAIR, FAR = 0, 1, 2, 3


PIECE = 64
RELAYED = 2

ORDER = (
    ("pair",0), ("pair",1), ("tokp",0), ("tokp",1), ("pair",2), ("tokp",2), ("tokp",3), ("tokp",4),
    ("tokp",5), ("tokp",6), ("tokp",7), ("tokp2",4), ("tokp2",5), ("tokp2",6), ("tokp2",7), ("near",0),
    ("near",1), ("near",2), ("src",0,0), ("tables",0), ("src",1,0), ("src",2,0), ("tables",1), ("w",0,0,2),
    ("src",0,2), ("w",0,0,1), ("src",0,1), ("w",0,1,0), ("w",0,2,0), ("w",1,0,2), ("src",1,2), ("w",1,0,1),
    ("w",1,1,0), ("w",1,2,0), ("t",0,0), ("w",2,0,1), ("w",2,1,0), ("w",2,2,0), ("w",0,0,3), ("w",0,1,2),
    ("w",0,2,2), ("w",0,1,1), ("w",0,2,1), ("w",0,3,0), ("w",0,4,0), ("t",0,1), ("sib",0,0), ("w",1,0,3),
    ("w",1,1,2), ("w",1,2,2), ("s",0,0), ("w",2,0,2), ("w",0,1,3), ("w",0,2,3), ("t",1,0), ("t",2,0),
    ("w",1,3,0), ("w",1,4,0), ("t",0,2), ("t",1,1), ("sib",1,0), ("t",2,1), ("sib",2,0), ("w",2,3,0),
    ("w",2,4,0), ("t",0,3), ("sib",0,1), ("w",0,3,2), ("w",0,4,2), ("w",0,3,1), ("w",0,4,1), ("w",1,1,3),
    ("w",0,5,0), ("w",0,6,0), ("s",1,0), ("s",2,0), ("t",0,4), ("s",0,1), ("t",3,0), ("w",1,2,3),
    ("src",1,1), ("w",1,3,2), ("w",1,4,2), ("t",2,2), ("t",0,5), ("sib",0,2), ("t",1,2), ("w",2,0,3),
    ("w",1,5,0), ("w",1,6,0), ("t",2,3), ("sib",2,1), ("w",0,3,3), ("w",0,4,3), ("dots",0,(0,1,2,3,4),0),
    ("s",0,2), ("t",0,6), ("t",3,1), ("sib",3,0), ("w",2,5,0), ("w",2,6,0), ("s",2,1), ("t",2,4),
    ("w",0,5,2), ("w",0,6,2), ("t",0,7), ("sib",0,3), ("w",0,5,1), ("w",0,6,1), ("w",0,7,0), ("w",0,8,0),
    ("w",1,3,3), ("t",1,3), ("sib",1,1), ("s",3,0), ("t",3,2), ("src",2,2), ("s",0,3), ("t",3,4),
    ("w",1,1,1), ("w",1,2,1), ("dots",0,(0,1,2),1), ("w",1,4,3), ("s",1,1), ("t",1,4), ("t",2,5),
    ("sib",2,2), ("w",0,5,3), ("w",0,6,3), ("dots",0,(5,6),0), ("t",3,5), ("sib",3,2), ("w",1,5,2),
    ("w",1,6,2), ("t",1,5), ("sib",1,2), ("s",2,2), ("t",3,3), ("sib",3,1), ("w",1,7,0), ("w",1,8,0),
    ("t",3,6), ("w",2,7,0), ("w",2,8,0), ("src",2,1), ("s",3,2), ("w",0,7,2), ("w",0,8,2), ("t",1,6),
    ("w",0,7,1), ("w",0,8,1), ("s",1,2), ("t",2,6), ("s",3,1), ("t",3,7), ("sib",3,3), ("t",1,7),
    ("sib",1,3), ("w",2,1,2), ("w",2,2,2), ("t",2,7), ("sib",2,3), ("w",1,5,3), ("s",3,3), ("s",1,3),
    ("w",1,3,1), ("w",1,4,1), ("dots",0,(3,4),1), ("s",2,3), ("dots",1,(0,1,2,3,4,5,6),0), ("w",1,6,3),
    ("w",1,7,2), ("w",1,8,2), ("w",0,7,3), ("w",0,8,3), ("dots",1,(7,),0), ("kv",1), ("w",2,1,1),
    ("w",2,2,1), ("w",2,1,3), ("dots",0,(7,),0), ("kv",0), ("dots",1,(0,1,2,3,4),1), ("w",2,3,2),
    ("w",2,4,2), ("w",2,2,3), ("dots",0,(0,1,2),2), ("w",1,7,3), ("w",1,5,1), ("w",1,6,1),
    ("dots",1,(5,6),1), ("dots",0,(5,6),1), ("w",1,8,3), ("w",2,3,1), ("w",2,4,1), ("w",2,5,2), ("w",2,3,3),
    ("w",2,6,2), ("w",1,7,1), ("w",1,8,1), ("dots",1,(7,),1), ("dots",0,(7,),1), ("kvin",1), ("att",1,1,0),
    ("w",2,4,3), ("att",1,1,1), ("w",2,5,1), ("w",2,6,1), ("dots",1,(0,1,2,3,4),2), ("kvin",0), ("w",2,7,2),
    ("w",2,8,2), ("dots",0,(3,4),2), ("w",2,5,3), ("att",0,1,0), ("att",0,1,1), ("w",2,6,3),
    ("dots",1,(5,6),2), ("w",2,7,1), ("w",2,8,1), ("dots",0,(5,6),2), ("w",2,7,3), ("w",2,8,3),
    ("dots",1,(7,),2), ("att",1,2,0), ("att",1,2,1), ("dots",0,(7,),2), ("att",0,2,0), ("att",0,2,1),
)


def kernel(tok, w, kvw, qg_in, kg_in, freq_in, dl_in, out,
           tokb, wbuf, kvbuf, stage, acc, kvacc, kvst, kvin, cosb, sinb, bias, ost, qg, kg, freq, dl,
           send, rw, rt, rs, rkv, rout, loc):
    dp = lax.axis_index("dp")
    hd = lax.axis_index("head")
    x, z = dp // 8, dp % 8
    y, c = hd // 2, hd % 2
    side = x // 2
    xn, xp = x + 1 - 2 * (x % 2), 3 - x
    worker = c == side
    is_v = y // 2
    kv_to = 2 * (y % 2) + side

    def dev(xx, zz, yy, cc):
        return (xx * 8 + zz, yy * 2 + cc)

    near = dev(xn, z, y, c)
    pair = dev(xp, z, y, c)
    up, down = dev(x, (z + 1) % 8, y, c), dev(x, (z + 7) % 8, y, c)
    yup, ydown = dev(x, z, (y + 1) % 4, c), dev(x, z, (y + 3) % 4, c)
    sib = dev(x, z, y, 1 - c)

    small = [pltpu.make_async_copy(a, b, loc.at[4 + n])
             for n, (a, b) in enumerate(((qg_in, qg), (kg_in, kg), (freq_in, freq), (dl_in, dl)))]

    def columns(of_side, g):
        return w.at[:, pl.ds(pl.multiple_of(of_side * 512 + (g - 1) * 256, 256), 256)]

    load_kv = pltpu.make_async_copy(kvw, kvbuf.at[0], loc.at[1])
    load_kv.start()
    for g in (1, 2):
        pltpu.make_async_copy(columns(side, g), wbuf.at[g - 1, 0], loc.at[2]).start()
        pltpu.make_async_copy(columns(1 - side, g), stage.at[g - 1], loc.at[2]).start()
    load_tok = pltpu.make_async_copy(tok, tokb.at[0], loc.at[0])
    load_tok.start()
    for copy in small:
        copy.start()

    barrier = pltpu.get_barrier_semaphore()
    for peer in (near, pair, up, down, yup, ydown, sib):
        pl.semaphore_signal(barrier, inc=1, device_id=peer, device_id_type=MESH)
    src_side = y % 2
    src_x = jnp.where(side == src_side, x, xp)
    kv_self = worker & (kv_to == y)
    for v in (0, 1):
        src_y = 2 * v + y // 2
        @pl.when((c == src_side) & jnp.logical_not(kv_self & (is_v == v)))
        def _():
            pl.semaphore_signal(
                barrier, inc=1, device_id=dev(src_x, z, src_y, src_side), device_id_type=MESH)
    extra = jnp.where(worker, jnp.where(kv_to == y, 1, 2), 0)
    pl.semaphore_wait(barrier, 7 + extra)

    def push(src, dst, rsem, to, sid):
        pltpu.make_async_remote_copy(
            src_ref=src, dst_ref=dst, send_sem=send.at[sid], recv_sem=rsem,
            device_id=to, device_id_type=MESH).start()

    def arrive(dst, sem):
        pltpu.make_async_copy(dst, dst, sem).wait()

    def group(g):
        return kvbuf if g == 0 else wbuf.at[g - 1]

    def slot(g, q, xi):
        if q < 7:
            return group(g).at[4 * q + xi]
        return group(g).at[28 + xi, pl.ds(64 * (q - 7), 64), :]

    def half(g, q, xi, h):
        return group(g).at[4 * q + xi, pl.ds(64 * h, 64), :]

    def place(g, q, xi):
        if xi == FAR:
            n, blocks = ((23, 3),) * 3 + ((24, 2),) * 2 + ((25, 2),) * 2 + ((26, 1),) * 2, None
            n, blocks = n[q]
            copies = 2 if blocks == 1 else blocks
        elif xi != PAIR and q >= 7:
            n, blocks, copies = 22, 2, 4
        else:
            n, blocks, copies = (q - 1, q + 6, q + 13)[xi], 1, 1
        return rw.at[g, n], n, blocks, copies

    def rsem_of(g, q, xi):
        return place(g, q, xi)[0]

    def guarded(g, fn):
        if g == 0:
            pl.when(worker)(fn)
        else:
            fn()

    arrivals = {}

    def counted(key, copies):
        arrivals[key] = arrivals.get(key, 0) + 1
        return arrivals[key] == copies

    def wait_w(g, q, xi):
        sem, n, blocks, copies = place(g, q, xi)
        if copies == 1:
            arrive(slot(g, q, xi), sem)
        elif counted((g, n), copies):
            arrive(group(g).at[pl.ds(0, blocks)], sem)

    def ring_start(g, xi):
        def go():
            for d, to in ((1, up), (2, down)):
                push(slot(g, 0, xi), slot(g, d, xi), rsem_of(g, d, xi), to, g)
        guarded(g, go)

    def cross(g, q):
        push(slot(g, q, PAIR), slot(g, q, FAR), rsem_of(g, q, FAR), near, g)

    def start_pair(g):
        if g == 0:
            @pl.when(jnp.logical_not(worker))
            def _():
                push(slot(0, 0, OWN), slot(0, 0, PAIR), rsem_of(0, 0, PAIR), pair, S_HELP)
        else:
            push(stage.at[g - 1], slot(g, 0, PAIR), rsem_of(g, 0, PAIR), pair, g)

    def start_near(g):
        def go():
            push(slot(g, 0, OWN), slot(g, 0, NEAR), rsem_of(g, 0, NEAR), near, g)
        guarded(g, go)

    def cols(head_of):
        return pl.ds(pl.multiple_of(head_of * 512, 512), 512)

    def piece(j, head_of):
        return tokb.at[1, pl.ds(PIECE * j, PIECE), cols(head_of)]

    y_of = (y, (y + 3) % 4, (y + 1) % 4, (y + 2) % 4)

    def tok_pair(s, j):
        of = y_of[s] * 2 + c
        src = tokb.at[0, pl.ds(PIECE * j, PIECE), cols(of)]
        push(src, piece(j, of), rt.at[s, j], pair, S_TOK)

    def tok_arrived(s, j):
        ref = piece(j, y_of[s] * 2 + c)
        arrive(ref, rt.at[s, j])
        if s == 0:
            push(ref, ref, rt.at[1, j], yup, S_TOK)
            push(ref, ref, rt.at[2, j], ydown, S_TOK)
        if s == 1 and j < RELAYED:
            push(ref, ref, rt.at[3, j], yup, S_TOK)
        if s == 2 and RELAYED <= j < 2 * RELAYED:
            push(ref, ref, rt.at[3, j], ydown, S_TOK)

    def quarter(b, head_of):
        return tokb.at[1, pl.ds(128 * b, 128), cols(head_of)]

    def to_sibling(s, b):
        ref = quarter(b, y_of[s] * 2 + c)
        push(ref, ref, rs.at[0], sib, S_TOK)

    def from_sibling(s, b):
        if counted("sibling", 16):
            arrive(tokb.at[1, pl.ds(0, 256), :], rs.at[0])

    def tables(t):
        rank = dp if t == 0 else xp * 8 + z
        row = lax.broadcasted_iota(jnp.int32, (ROWS, HD), 0)
        lane = lax.broadcasted_iota(jnp.int32, (ROWS, HD), 1)
        start = jnp.zeros((ROWS, HD), jnp.int32)
        end = 0
        for d in range(16):
            n = dl[d, rank]
            end = end + n
            start = start + jnp.where(row >= end, n, 0)
        angle = (row - start).astype(F32) * freq[...]
        cosb[t] = jnp.cos(angle)
        s = jnp.sin(angle)
        sinb[t] = jnp.where(lane < 64, -s, s)
        for j in range(4):
            col = lane + 128 * j
            bias[t, :, 128 * j:128 * j + 128] = jnp.where(
                (col >= start) & (col <= row), 0.0, -1e30)

    def norm_rope(u, gain, t):
        ms = jnp.mean(u * u, axis=-1, keepdims=True)
        n = u * lax.rsqrt(ms + EPS) * gain
        return (n * cosb[t] + pltpu.roll(n, 64, 1) * sinb[t]).astype(BF16)

    def lhs(t, ps):
        parts = []
        for p in ps:
            zz = (z + 8 + (-1 if p % 2 else 1) * ((p + 1) // 2)) % 8
            for xx in (x, xn, xp, 3 - xn):
                f = pl.multiple_of((xx * 8 + zz) * 128, 128)
                parts.append(tokb[t, :, pl.ds(f, 128)])
        return jnp.concatenate(parts, axis=1)

    def dots(t, ps, g):
        def go():
            width = 128 if g == 0 else 256
            b = group(g)[pl.ds(4 * ps[0], 4 * len(ps))].reshape(512 * len(ps), width)
            total = kvacc.at[t] if g == 0 else acc.at[t, g - 1]
            new = jnp.dot(lhs(t, ps), b, preferred_element_type=F32)
            total[...] = new if ps[0] == 0 else total[...] + new
        guarded(g, go)

    def kv_finish(t):
        @pl.when(worker & (is_v == 0))
        def _():
            kvst[t] = norm_rope(kvacc[t], kg[...], t)

        @pl.when(worker & (is_v == 1))
        def _():
            kvst[t] = kvacc[t].astype(BF16)

    def kv_send(t):
        def send_to(xx, tt, sid):
            push(kvst.at[t], kvin.at[is_v, tt], rkv.at[tt], dev(xx, z, kv_to, c), sid)

        pl.when(worker)(lambda: send_to(xp, 1 - t, S_KEYS))
        pl.when(worker & (kv_to != y))(lambda: send_to(x, t, S_BEYOND))

        @pl.when(worker & (kv_to == y))
        def _():
            pltpu.make_async_copy(kvst.at[t], kvin.at[is_v, t], rkv.at[t]).start()

    first_core = c == y % 2

    def kv_arrived(t):
        arrive(kvst, rkv.at[t])

        @pl.when(first_core)
        def _():
            push(kvin.at[:, t], kvin.at[:, t], rkv.at[t], sib, S_SHARE)

    scale = HD ** -0.5 * math.log2(math.e)

    def attend(t, g, hh):
        q = norm_rope(acc[t, g - 1, :, 128 * hh:128 * hh + 128], qg[...], t)
        for i in (0, 1):
            m = 256 * (i + 1)
            s = lax.dot_general(q[256 * i:m], kvin[0, t, :m], (((1,), (1,)), ((), ())),
                                preferred_element_type=F32)
            e = jnp.exp2(s * scale + bias[t, 256 * i:m, :m]).astype(BF16)
            v = jnp.concatenate([kvin[1, t, :m], jnp.ones((m, HD), BF16)], axis=1)
            o = jnp.dot(e, v, preferred_element_type=F32)
            at = (g - 1) * 256 + 128 * hh
            ost[t, 256 * i:m, at:at + 128] = (o[:, :HD] / o[:, HD:]).astype(BF16)

    def emit(t, g, hh):
        at = (g - 1) * 256 + hh * 128
        here = ost.at[t, :, pl.ds(at, 128)]
        there = out.at[:, pl.ds(pl.multiple_of(side * 512 + at, 128), 128)]
        if t == 1:
            push(here, there, rout.at[0], pair, S_OUT)
        else:
            pltpu.make_async_copy(here, there, loc.at[3]).start()

    def weights(g, q, xi):
        def go():
            wait_w(g, q, xi)
            if 0 < q < 7 and xi != FAR:
                d = (q + 1) % 2
                src = slot(g, q, xi) if q < 5 else half(g, q, xi, d)
                on = q + 2
                push(src, slot(g, on, xi), rsem_of(g, on, xi), (up, down)[d], g)
            if xi == PAIR:
                cross(g, q)
        guarded(g, go)

    load_kv.wait()
    arrive(wbuf.at[0, pl.ds(0, 4)], loc.at[2])
    once = set()

    def first(name):
        new = name not in once
        once.add(name)
        return new

    for what, *a in ORDER:
        if what == "tables" and first("small"):
            for copy in small:
                copy.wait()
        if what in ("dots", "tokp") and first("tok"):
            load_tok.wait()
        if what == "near":
            start_near(*a)
        elif what == "pair":
            start_pair(*a)
        elif what == "tokp":
            tok_pair(0, *a)
        elif what == "tokp2":
            tok_pair(3, *a)
        elif what == "src":
            ring_start(*a)
        elif what == "w":
            weights(*a)
        elif what == "t":
            tok_arrived(*a)
        elif what == "sib":
            to_sibling(*a)
        elif what == "s":
            from_sibling(*a)
        elif what == "tables":
            tables(*a)
        elif what == "dots":
            dots(*a)
        elif what == "kv":
            kv_finish(*a)
            kv_send(*a)
        elif what == "kvin":
            kv_arrived(*a)
        elif what == "att":
            attend(*a)
            emit(*a)

    for g in (1, 2):
        arrive(group(g).at[pl.ds(0, 31)], send.at[g])
    arrive(tokb.at[1], send.at[S_TOK])
    arrive(ost.at[0], send.at[S_OUT])

    @pl.when(worker)
    def _():
        arrive(kvbuf.at[pl.ds(0, 30)], send.at[S_KV])
        arrive(kvst, send.at[S_KEYS])

    @pl.when(first_core)
    def _():
        arrive(kvin, send.at[S_SHARE])

    @pl.when(worker & (kv_to != y))
    def _():
        arrive(kvst, send.at[S_BEYOND])

    @pl.when(jnp.logical_not(worker))
    def _():
        arrive(kvbuf.at[0], send.at[S_HELP])

    arrive(ost.at[0], loc.at[3])
    arrive(ost.at[1], rout.at[0])


def shards(tokens, q_weight, kv_weight, q_gain, k_gain, doc_lengths):
    half = np.exp(np.arange(64) * (-2.0 * math.log(THETA) / HD)).astype(np.float32)
    freq = jnp.asarray(np.concatenate([half, half])[None, :])
    any_ = pl.BlockSpec(memory_space=pl.ANY)
    dma = pltpu.SemaphoreType.DMA
    return pl.pallas_call(
        kernel,
        out_shape=jax.ShapeDtypeStruct((ROWS, 1024), BF16),
        in_specs=[any_] * 7,
        out_specs=any_,
        scratch_shapes=[
            pltpu.VMEM((2, ROWS, FEAT), BF16),
            pltpu.VMEM((2, 32, 128, 256), BF16),
            pltpu.VMEM((32, 128, 128), BF16),
            pltpu.VMEM((2, 128, 256), BF16),
            pltpu.VMEM((2, 2, ROWS, 256), F32),
            pltpu.VMEM((2, ROWS, 128), F32),
            pltpu.VMEM((2, ROWS, 128), BF16),
            pltpu.VMEM((2, 2, ROWS, 128), BF16),
            pltpu.VMEM((2, ROWS, HD), F32),
            pltpu.VMEM((2, ROWS, HD), F32),
            pltpu.VMEM((2, ROWS, ROWS), F32),
            pltpu.VMEM((2, ROWS, 512), BF16),
            pltpu.VMEM((1, HD), F32),
            pltpu.VMEM((1, HD), F32),
            pltpu.VMEM((1, HD), F32),
            pltpu.SMEM((16, 32), jnp.int32),
            dma((9,)),
            dma((3, 27)),
            dma((4, 8)),
            dma((1,)),
            dma((2,)),
            dma((1,)),
            dma((8,)),
        ],
        compiler_params=pltpu.CompilerParams(
            collective_id=0, has_side_effects=True, vmem_limit_bytes=60 * 2**20),
        cost_estimate=pl.CostEstimate(
            flops=6_000_000_000, bytes_accessed=12 * 2**20, transcendentals=2**21),
    )(tokens, q_weight, kv_weight, q_gain[None, :], k_gain[None, :], freq, doc_lengths.T)


def solution(mesh):
    placed = (P("dp", None), P("dp", "head"), P("dp", "head"), P(), P(), P())
    return jax.shard_map(
        shards, mesh=mesh, in_specs=placed, out_specs=P("dp", "head"), check_vma=False
    )
```

```python
import functools
import math

import jax
import jax.numpy as jnp
import numpy as np
from jax import lax
from jax.experimental import pallas as pl
from jax.experimental.pallas import tpu as pltpu
from jax.sharding import PartitionSpec as P

HD = 128
ROWS = 512
FEAT = 4096
THETA = 1000000.0
EPS = 1e-06
MESH = pl.DeviceIdType.MESH
F32 = jnp.float32
BF16 = jnp.bfloat16
S_KV, S_HELP, S_TOK, S_KEYS, S_BEYOND, S_QUERY = 0, 3, 4, 5, 6, 7
GROUPS = (0, 1, 2)
OWN, NEAR, PAIR, FAR = 0, 1, 2, 3


PIECE = 64
RELAYED = 2

ORDER = (
    ("pair",0), ("near",0), ("pair",1), ("tokp",0), ("src",2,0), ("w",2,8,0), ("tables",0), ("near",2),
    ("w",0,0,3), ("src",1,0), ("near",1), ("s",3,0), ("src",0,0), ("tokp",1), ("tokp2",7), ("w",2,2,0),
    ("tokp",3), ("tokp",2), ("w",2,7,0), ("w",0,0,2), ("s",2,3), ("tokp",4), ("w",1,0,2), ("w",0,0,1),
    ("tokp",6), ("src",0,2), ("pair",2), ("s",2,2), ("src",1,2), ("src",0,1), ("w",2,1,0), ("t",0,0),
    ("tables",1), ("w",0,2,0), ("w",0,1,0), ("w",1,1,0), ("w",1,2,0), ("tokp",5), ("w",2,1,3), ("w",2,0,1),
    ("tokp2",4), ("w",0,7,3), ("t",0,1), ("w",0,1,2), ("tokp2",5), ("src",2,1), ("w",0,2,2), ("t",2,0),
    ("w",1,0,1), ("w",0,2,1), ("w",0,1,1), ("t",0,2), ("sib",0,0), ("t",1,0), ("tokp",7), ("t",0,3),
    ("w",1,1,2), ("w",0,5,3), ("w",1,2,2), ("src",1,1), ("w",0,3,2), ("w",0,3,0), ("w",0,4,0), ("t",2,1),
    ("w",2,4,0), ("w",0,4,2), ("w",1,2,3), ("t",0,4), ("w",2,0,3), ("tokp2",6), ("w",1,4,3), ("w",1,4,0),
    ("w",0,4,1), ("w",1,1,3), ("w",1,3,0), ("w",0,3,1), ("s",2,1), ("t",2,2), ("w",1,5,3), ("w",1,4,2),
    ("s",1,0), ("t",0,6), ("w",1,0,3), ("w",0,2,3), ("t",1,1), ("w",0,4,3), ("w",1,3,2), ("s",0,3),
    ("s",1,1), ("w",2,0,2), ("w",1,7,3), ("src",2,2), ("t",0,5), ("w",0,5,0), ("t",3,4), ("t",1,2),
    ("w",0,6,2), ("t",1,3), ("w",0,7,0), ("w",0,5,2), ("w",2,6,0), ("sib",0,2), ("t",2,3), ("w",2,3,0),
    ("w",0,3,3), ("w",0,1,3), ("w",1,7,0), ("t",2,4), ("w",1,2,1), ("s",1,2), ("sib",2,0), ("s",3,3),
    ("sib",2,1), ("w",1,1,1), ("dots",0,(0,1,2,3,4),0), ("t",0,7), ("w",1,5,2), ("s",3,1), ("t",3,7),
    ("sib",0,3), ("w",0,5,1), ("w",0,8,1), ("t",3,0), ("dots",0,(0,1,2),1), ("t",1,4), ("w",0,6,0),
    ("t",3,1), ("sib",1,0), ("w",1,6,2), ("sib",1,1), ("t",2,5), ("s",2,0), ("s",0,2), ("w",0,8,0),
    ("w",0,6,1), ("w",2,3,3), ("s",0,0), ("sib",3,0), ("sib",0,1), ("w",0,7,2), ("t",3,5), ("s",3,2),
    ("t",1,5), ("w",0,8,2), ("t",3,6), ("w",0,6,3), ("sib",3,2), ("w",2,7,1), ("w",2,1,2), ("t",3,3),
    ("w",2,1,1), ("w",2,2,2), ("w",1,3,3), ("w",2,2,1), ("dots",0,(5,6),0), ("sib",2,2), ("t",1,6),
    ("t",3,2), ("sib",3,1), ("sib",1,2), ("sib",3,3), ("t",2,6), ("t",1,7), ("sib",1,3), ("t",2,7),
    ("w",2,5,3), ("s",0,1), ("w",1,4,1), ("w",1,3,1), ("sib",2,3), ("w",1,7,2), ("w",1,8,2), ("s",1,3),
    ("dots",1,(0,1,2,3,4,5,6),0), ("w",2,4,2), ("w",0,8,3), ("w",2,3,2), ("w",0,7,1), ("dots",1,(7,),0),
    ("w",1,6,0), ("kv",1), ("w",1,6,3), ("w",2,3,1), ("w",1,8,0), ("w",2,4,1), ("dots",1,(0,1,2,3,4),1),
    ("w",1,5,0), ("w",1,6,1), ("dots",0,(7,),0), ("w",1,5,1), ("kv",0), ("w",2,2,3), ("w",2,5,2),
    ("w",2,6,2), ("dots",1,(5,6),1), ("w",2,5,1), ("w",1,7,1), ("dots",0,(0,1,2),2), ("w",2,5,0),
    ("dots",0,(3,4),1), ("w",1,8,3), ("w",1,8,1), ("dots",1,(7,),1), ("q",1), ("w",2,6,1),
    ("dots",0,(5,6),1), ("w",2,8,2), ("dots",0,(7,),1), ("w",2,4,3), ("w",2,7,2), ("dots",1,(0,1,2,3,4),2),
    ("w",2,6,3), ("dots",0,(3,4),2), ("w",2,8,3), ("dots",1,(5,6),2), ("w",2,7,3), ("w",2,8,1),
    ("dots",1,(7,),2), ("q",2), ("dots",0,(5,6),2), ("qin",1,0), ("dots",0,(7,),2), ("kvin",), ("qin",1,1),
    ("att",1,1), ("att",0,2), ("att",0,1), ("qin",2,0), ("att",1,2,0), ("qin",2,1), ("att",1,2,1),
)


def kernel(tok, w, kvw, qg_in, kg_in, freq_in, dl_in, out,
           tokb, wbuf, kvbuf, stage, acc, kvacc, kvst, kvin, cosb, sinb, bias, ost, qst, qin, qg, kg, freq, dl,
           send, rw, rt, rs, rkv, rq, loc):
    dp = lax.axis_index("dp")
    hd = lax.axis_index("head")
    x, z = dp // 8, dp % 8
    y, c = hd // 2, hd % 2
    side = x // 2
    xn, xp = x + 1 - 2 * (x % 2), 3 - x
    worker = c == side
    is_v = y // 2
    kv_to = 2 * (y % 2) + side

    def dev(xx, zz, yy, cc):
        return (xx * 8 + zz, yy * 2 + cc)

    near = dev(xn, z, y, c)
    pair = dev(xp, z, y, c)
    up, down = dev(x, (z + 1) % 8, y, c), dev(x, (z + 7) % 8, y, c)
    yup, ydown = dev(x, z, (y + 1) % 4, c), dev(x, z, (y + 3) % 4, c)
    sib = dev(x, z, y, 1 - c)

    small = [pltpu.make_async_copy(a, b, loc.at[4 + n])
             for n, (a, b) in enumerate(((qg_in, qg), (kg_in, kg), (freq_in, freq), (dl_in, dl)))]

    def columns(of_side, g):
        return w.at[:, pl.ds(pl.multiple_of(of_side * 512 + (g - 1) * 256, 256), 256)]

    load_kv = pltpu.make_async_copy(kvw, kvbuf.at[0], loc.at[1])
    load_kv.start()
    for g in (1, 2):
        pltpu.make_async_copy(columns(side, g), wbuf.at[g - 1, 0], loc.at[2]).start()
        pltpu.make_async_copy(columns(1 - side, g), stage.at[g - 1], loc.at[2]).start()
    load_tok = pltpu.make_async_copy(tok, tokb.at[0], loc.at[0])
    load_tok.start()
    for copy in small:
        copy.start()

    barrier = pltpu.get_barrier_semaphore()
    for peer in (near, pair, up, down, yup, ydown, sib):
        pl.semaphore_signal(barrier, inc=1, device_id=peer, device_id_type=MESH)
    src_side = y % 2
    src_x = jnp.where(side == src_side, x, xp)
    kv_self = worker & (kv_to == y)
    for v in (0, 1):
        src_y = 2 * v + y // 2
        @pl.when(jnp.logical_not(kv_self & (is_v == v)))
        def _():
            pl.semaphore_signal(
                barrier, inc=1, device_id=dev(src_x, z, src_y, src_side), device_id_type=MESH)
    extra = jnp.where(worker, jnp.where(kv_to == y, 3, 4), 0)
    pl.semaphore_wait(barrier, 7 + extra)

    def push(src, dst, rsem, to, sid):
        pltpu.make_async_remote_copy(
            src_ref=src, dst_ref=dst, send_sem=send.at[sid], recv_sem=rsem,
            device_id=to, device_id_type=MESH).start()

    def arrive(dst, sem):
        pltpu.make_async_copy(dst, dst, sem).wait()

    def group(g):
        return kvbuf if g == 0 else wbuf.at[g - 1]

    def slot(g, q, xi):
        if q < 7:
            return group(g).at[4 * q + xi]
        return group(g).at[28 + xi, pl.ds(64 * (q - 7), 64), :]

    def half(g, q, xi, h):
        return group(g).at[4 * q + xi, pl.ds(64 * h, 64), :]

    def place(g, q, xi):
        if xi == FAR:
            n, blocks = ((23, 3),) * 3 + ((24, 2),) * 2 + ((25, 2),) * 2 + ((26, 1),) * 2, None
            n, blocks = n[q]
            copies = 2 if blocks == 1 else blocks
        elif xi != PAIR and q >= 7:
            n, blocks, copies = 22, 2, 4
        else:
            n, blocks, copies = (q - 1, q + 6, q + 13)[xi], 1, 1
        return rw.at[g, n], n, blocks, copies

    def rsem_of(g, q, xi):
        return place(g, q, xi)[0]

    def guarded(g, fn):
        if g == 0:
            pl.when(worker)(fn)
        else:
            fn()

    arrivals = {}

    def counted(key, copies):
        arrivals[key] = arrivals.get(key, 0) + 1
        return arrivals[key] == copies

    def wait_w(g, q, xi):
        sem, n, blocks, copies = place(g, q, xi)
        if copies == 1:
            arrive(slot(g, q, xi), sem)
        elif counted((g, n), copies):
            arrive(group(g).at[pl.ds(0, blocks)], sem)

    def ring_start(g, xi):
        def go():
            for d, to in ((1, up), (2, down)):
                push(slot(g, 0, xi), slot(g, d, xi), rsem_of(g, d, xi), to, g)
        guarded(g, go)

    def cross(g, q):
        push(slot(g, q, PAIR), slot(g, q, FAR), rsem_of(g, q, FAR), near, g)

    def start_pair(g):
        if g == 0:
            @pl.when(jnp.logical_not(worker))
            def _():
                push(slot(0, 0, OWN), slot(0, 0, PAIR), rsem_of(0, 0, PAIR), pair, S_HELP)
        else:
            push(stage.at[g - 1], slot(g, 0, PAIR), rsem_of(g, 0, PAIR), pair, g)

    def start_near(g):
        def go():
            push(slot(g, 0, OWN), slot(g, 0, NEAR), rsem_of(g, 0, NEAR), near, g)
        guarded(g, go)

    def cols(head_of):
        return pl.ds(pl.multiple_of(head_of * 512, 512), 512)

    def piece(j, head_of):
        return tokb.at[1, pl.ds(PIECE * j, PIECE), cols(head_of)]

    y_of = (y, (y + 3) % 4, (y + 1) % 4, (y + 2) % 4)

    def tok_pair(s, j):
        of = y_of[s] * 2 + c
        src = tokb.at[0, pl.ds(PIECE * j, PIECE), cols(of)]
        push(src, piece(j, of), rt.at[s, j], pair, S_TOK)

    def tok_arrived(s, j):
        ref = piece(j, y_of[s] * 2 + c)
        arrive(ref, rt.at[s, j])
        if s == 0:
            push(ref, ref, rt.at[1, j], yup, S_TOK)
            push(ref, ref, rt.at[2, j], ydown, S_TOK)
        if s == 1 and j < RELAYED:
            push(ref, ref, rt.at[3, j], yup, S_TOK)
        if s == 2 and RELAYED <= j < 2 * RELAYED:
            push(ref, ref, rt.at[3, j], ydown, S_TOK)

    def quarter(b, head_of):
        return tokb.at[1, pl.ds(128 * b, 128), cols(head_of)]

    def to_sibling(s, b):
        ref = quarter(b, y_of[s] * 2 + c)
        push(ref, ref, rs.at[0], sib, S_TOK)

    def from_sibling(s, b):
        if counted("sibling", 16):
            arrive(tokb.at[1, pl.ds(0, 256), :], rs.at[0])

    def tables(t):
        rank = dp if t == 0 else xp * 8 + z
        row = lax.broadcasted_iota(jnp.int32, (ROWS, HD), 0)
        lane = lax.broadcasted_iota(jnp.int32, (ROWS, HD), 1)
        start = jnp.zeros((ROWS, HD), jnp.int32)
        end = 0
        for d in range(16):
            n = dl[d, rank]
            end = end + n
            start = start + jnp.where(row >= end, n, 0)
        angle = (row - start).astype(F32) * freq[...]
        cosb[t] = jnp.cos(angle)
        s = jnp.sin(angle)
        sinb[t] = jnp.where(lane < 64, -s, s)
        for j in range(4 if t == 0 else 0):
            col = lane + 128 * j
            bias[:, 128 * j:128 * j + 128] = jnp.where((col >= start) & (col <= row), 0.0, -1e30)

    def norm_rope(u, gain, t, by_matrix_unit=False):
        square = u * u
        if by_matrix_unit:
            high = square.astype(BF16)
            low = (square - high.astype(F32)).astype(BF16)
            ms = jnp.dot(jnp.concatenate([high, low], axis=1), jnp.full((2 * HD, HD), 1.0 / HD, BF16),
                         preferred_element_type=F32)
        else:
            ms = jnp.mean(square, axis=-1, keepdims=True)
        n = u * lax.rsqrt(ms + EPS) * gain
        return (n * cosb[t] + pltpu.roll(n, 64, 1) * sinb[t]).astype(BF16)

    def lhs(t, ps):
        parts = []
        for p in ps:
            zz = (z + 8 + (-1 if p % 2 else 1) * ((p + 1) // 2)) % 8
            for xx in (x, xn, xp, 3 - xn):
                f = pl.multiple_of((xx * 8 + zz) * 128, 128)
                parts.append(tokb[t, :, pl.ds(f, 128)])
        return jnp.concatenate(parts, axis=1)

    def dots(t, ps, g):
        def go():
            width = 128 if g == 0 else 256
            b = group(g)[pl.ds(4 * ps[0], 4 * len(ps))].reshape(512 * len(ps), width)
            total = kvacc.at[t] if g == 0 else acc.at[t, g - 1]
            new = jnp.dot(lhs(t, ps), b, preferred_element_type=F32)
            total[...] = new if ps[0] == 0 else total[...] + new
        guarded(g, go)

    def kv_finish(t):
        @pl.when(worker & (is_v == 0))
        def _():
            kvst[t] = norm_rope(kvacc[t], kg[...], t)

        @pl.when(worker & (is_v == 1))
        def _():
            kvst[t] = kvacc[t].astype(BF16)

    def kv_send(t):
        def send_to(xx, core, sid):
            push(kvst.at[t], kvin.at[is_v], rkv.at[0], dev(xx, z, kv_to, core), sid)

        @pl.when(worker)
        def _():
            if t == 1:
                send_to(xp, c, S_KEYS)
                send_to(xp, 1 - c, S_KEYS)
            else:
                send_to(x, 1 - c, S_KEYS)

        if t == 1:
            return
        pl.when(worker & (kv_to != y))(lambda: send_to(x, c, S_BEYOND))

        @pl.when(worker & (kv_to == y))
        def _():
            pltpu.make_async_copy(kvst.at[t], kvin.at[is_v], rkv.at[0]).start()

    def kv_arrived():
        arrive(kvin, rkv.at[0])

    scale = HD ** -0.5 * math.log2(math.e)

    def query(t, g, hh):
        u = acc[t, g - 1, :, 128 * hh:128 * hh + 128]
        return norm_rope(u, qg[...], t, by_matrix_unit=t == 0)

    def send_queries(g):
        for hh in (0, 1):
            n = 2 * (g - 1) + hh
            qst[n] = query(1, g, hh)
            push(qst.at[n], qin.at[n], rq.at[n], pair, S_QUERY)

    def attend(of, g, hh):
        n = 2 * (g - 1) + hh
        q = query(0, g, hh) if of == 0 else qin[n]
        for i in (0, 1):
            m = 256 * (i + 1)
            s = lax.dot_general(q[256 * i:m], kvin[0, :m], (((1,), (1,)), ((), ())),
                                preferred_element_type=F32)
            e = jnp.exp2(s * scale + bias[256 * i:m, :m]).astype(BF16)
            v = jnp.concatenate([kvin[1, :m], jnp.ones((m, HD), BF16)], axis=1)
            o = jnp.dot(e, v, preferred_element_type=F32)
            ost[of, 256 * i:m, 128 * n:128 * n + 128] = (o[:, :HD] / o[:, HD:]).astype(BF16)

    def emit(of, g, hh):
        at = 128 * (2 * (g - 1) + hh)
        first_col = (side if of == 0 else 1 - side) * 512 + at
        pltpu.make_async_copy(ost.at[of, :, pl.ds(at, 128)],
                              out.at[:, pl.ds(pl.multiple_of(first_col, 128), 128)], loc.at[3]).start()

    def weights(g, q, xi):
        def go():
            wait_w(g, q, xi)
            if 0 < q < 7 and xi != FAR:
                d = (q + 1) % 2
                src = slot(g, q, xi) if q < 5 else half(g, q, xi, d)
                on = q + 2
                push(src, slot(g, on, xi), rsem_of(g, on, xi), (up, down)[d], g)
            if xi == PAIR:
                cross(g, q)
        guarded(g, go)

    load_kv.wait()
    arrive(wbuf.at[0, pl.ds(0, 4)], loc.at[2])
    once = set()

    def first(name):
        new = name not in once
        once.add(name)
        return new

    for what, *a in ORDER:
        if what == "tables" and first("small"):
            for copy in small:
                copy.wait()
        if what in ("dots", "tokp", "tokp2") and first("tok"):
            load_tok.wait()
        if what == "near":
            start_near(*a)
        elif what == "pair":
            start_pair(*a)
        elif what == "tokp":
            tok_pair(0, *a)
        elif what == "tokp2":
            tok_pair(3, *a)
        elif what == "src":
            ring_start(*a)
        elif what == "w":
            weights(*a)
        elif what == "t":
            tok_arrived(*a)
        elif what == "sib":
            to_sibling(*a)
        elif what == "s":
            from_sibling(*a)
        elif what == "tables":
            tables(*a)
        elif what == "dots":
            dots(*a)
        elif what == "kv":
            kv_finish(*a)
            kv_send(*a)
        elif what == "kvin":
            kv_arrived()
        elif what == "q":
            send_queries(*a)
        elif what == "qin":
            n = 2 * (a[0] - 1) + a[1]
            arrive(qin.at[n], rq.at[n])
        elif what == "att":
            heads = (0, 1) if len(a) == 2 else a[2:]
            for hh in heads:
                attend(a[0], a[1], hh)
            for hh in heads:
                emit(a[0], a[1], hh)

    for g in (1, 2):
        arrive(group(g).at[pl.ds(0, 31)], send.at[g])
    arrive(tokb.at[1], send.at[S_TOK])
    arrive(qst, send.at[S_QUERY])

    @pl.when(worker)
    def _():
        arrive(kvbuf.at[pl.ds(0, 30)], send.at[S_KV])
        arrive(wbuf.at[0, pl.ds(0, 6)], send.at[S_KEYS])

    @pl.when(worker & (kv_to != y))
    def _():
        arrive(kvst.at[0], send.at[S_BEYOND])

    @pl.when(jnp.logical_not(worker))
    def _():
        arrive(kvbuf.at[0], send.at[S_HELP])

    arrive(ost, loc.at[3])


def shards(tokens, q_weight, kv_weight, q_gain, k_gain, doc_lengths):
    half = np.exp(np.arange(64) * (-2.0 * math.log(THETA) / HD)).astype(np.float32)
    freq = jnp.asarray(np.concatenate([half, half])[None, :])
    any_ = pl.BlockSpec(memory_space=pl.ANY)
    dma = pltpu.SemaphoreType.DMA
    return pl.pallas_call(
        kernel,
        out_shape=jax.ShapeDtypeStruct((ROWS, 1024), BF16),
        in_specs=[any_] * 7,
        out_specs=any_,
        scratch_shapes=[
            pltpu.VMEM((2, ROWS, FEAT), BF16),
            pltpu.VMEM((2, 32, 128, 256), BF16),
            pltpu.VMEM((32, 128, 128), BF16),
            pltpu.VMEM((2, 128, 256), BF16),
            pltpu.VMEM((2, 2, ROWS, 256), F32),
            pltpu.VMEM((2, ROWS, 128), F32),
            pltpu.VMEM((2, ROWS, 128), BF16),
            pltpu.VMEM((2, ROWS, 128), BF16),
            pltpu.VMEM((2, ROWS, HD), F32),
            pltpu.VMEM((2, ROWS, HD), F32),
            pltpu.VMEM((ROWS, ROWS), F32),
            pltpu.VMEM((2, ROWS, 512), BF16),
            pltpu.VMEM((4, ROWS, HD), BF16),
            pltpu.VMEM((4, ROWS, HD), BF16),
            pltpu.VMEM((1, HD), F32),
            pltpu.VMEM((1, HD), F32),
            pltpu.VMEM((1, HD), F32),
            pltpu.SMEM((16, 32), jnp.int32),
            dma((8,)),
            dma((3, 27)),
            dma((4, 8)),
            dma((1,)),
            dma((1,)),
            dma((4,)),
            dma((8,)),
        ],
        compiler_params=pltpu.CompilerParams(
            collective_id=0, has_side_effects=True, vmem_limit_bytes=60 * 2**20),
        cost_estimate=pl.CostEstimate(
            flops=6_000_000_000, bytes_accessed=12 * 2**20, transcendentals=2**21),
    )(tokens, q_weight, kv_weight, q_gain[None, :], k_gain[None, :], freq, doc_lengths.T)


def solution(mesh):
    placed = (P("dp", None), P("dp", "head"), P("dp", "head"), P(), P(), P())
    return jax.shard_map(
        shards, mesh=mesh, in_specs=placed, out_specs=P("dp", "head"), check_vma=False
    )
```

```python
import functools
import math

import jax
import jax.numpy as jnp
import numpy as np
from jax import lax
from jax.experimental import pallas as pl
from jax.experimental.pallas import tpu as pltpu
from jax.sharding import PartitionSpec as P

HD = 128
ROWS = 512
FEAT = 4096
THETA = 1000000.0
EPS = 1e-06
MESH = pl.DeviceIdType.MESH
F32 = jnp.float32
BF16 = jnp.bfloat16
S_KV, S_HELP, S_TOK, S_KEYS, S_BEYOND, S_QUERY = 0, 3, 4, 5, 6, 7
GROUPS = (0, 1, 2)
OWN, NEAR, PAIR, FAR = 0, 1, 2, 3


PIECE = 64
RELAYED = 2

ORDER = (
    ("w",0,2,3), ("w",2,8,0), ("w",0,5,3), ("w",2,5,3), ("pair",0), ("s",3,2), ("w",1,1,3), ("s",2,3),
    ("near",0), ("pair",1), ("src",2,0), ("near",2), ("s",1,0), ("tables",1), ("pair",2), ("s",1,2),
    ("src",0,0), ("src",1,0), ("w",0,0,2), ("src",0,2), ("w",1,2,3), ("tokp",3), ("tokp",0), ("near",1),
    ("w",0,8,0), ("w",0,2,0), ("w",1,0,2), ("src",1,2), ("w",2,0,2), ("w",0,0,1), ("w",2,7,0), ("src",0,1),
    ("w",2,0,1), ("w",0,1,0), ("tokp",2), ("src",2,2), ("w",1,2,0), ("tokp",1), ("w",2,1,0), ("w",0,0,3),
    ("s",2,0), ("t",0,3), ("s",1,1), ("w",0,1,2), ("tokp",4), ("t",0,0), ("w",0,2,2), ("w",2,2,0),
    ("w",1,1,2), ("w",1,1,0), ("w",1,0,1), ("s",0,0), ("w",1,2,2), ("w",1,3,3), ("tokp",7), ("w",0,3,0),
    ("tokp",6), ("t",0,2), ("w",0,1,1), ("s",0,3), ("t",0,1), ("src",1,1), ("tokp2",6), ("w",1,3,2),
    ("w",0,2,1), ("tokp",5), ("s",3,1), ("w",0,3,2), ("s",2,1), ("w",0,4,2), ("src",2,1), ("t",1,0),
    ("t",0,4), ("tokp2",7), ("t",2,2), ("t",2,3), ("s",3,0), ("w",0,4,0), ("w",1,4,2), ("s",2,2),
    ("w",1,4,0), ("t",1,1), ("w",0,3,1), ("w",2,1,2), ("tokp2",5), ("w",2,0,3), ("w",1,1,1), ("tokp2",4),
    ("w",0,6,2), ("w",0,4,1), ("s",1,3), ("w",2,7,1), ("w",2,3,3), ("w",1,2,1), ("w",0,7,1), ("t",0,6),
    ("sib",0,0), ("w",1,8,0), ("t",0,7), ("w",1,0,3), ("w",2,2,2), ("w",2,7,3), ("w",0,5,2), ("w",1,5,2),
    ("w",1,3,0), ("w",2,2,1), ("t",0,5), ("w",1,8,3), ("sib",1,0), ("tables",0), ("w",2,1,1), ("w",1,7,1),
    ("t",1,6), ("t",1,2), ("s",0,1), ("t",3,3), ("t",3,5), ("w",0,5,0), ("t",3,2), ("s",3,3), ("sib",0,2),
    ("t",1,3), ("t",2,4), ("t",3,0), ("sib",3,1), ("t",2,6), ("w",0,5,1), ("w",2,2,3), ("w",1,6,2),
    ("sib",1,1), ("w",0,8,2), ("t",3,1), ("t",1,4), ("t",2,1), ("w",0,6,1), ("w",0,3,3), ("sib",3,0),
    ("w",0,7,3), ("w",0,1,3), ("sib",0,1), ("t",3,4), ("w",0,6,0), ("sib",3,2), ("w",2,3,2), ("t",2,7),
    ("w",1,6,0), ("w",1,7,0), ("sib",2,3), ("w",2,1,3), ("w",1,3,1), ("t",1,7), ("sib",2,1), ("sib",0,3),
    ("t",3,7), ("t",1,5), ("w",0,7,2), ("t",2,5), ("t",3,6), ("sib",2,2), ("t",2,0), ("w",1,4,1),
    ("w",0,6,3), ("sib",2,0), ("sib",3,3), ("w",0,4,3), ("sib",1,3), ("w",1,7,2), ("sib",1,2), ("w",1,6,3),
    ("w",1,4,3), ("dots",0,(0,1,2),1), ("dots",0,(0,1,2,3,4),0), ("dots",0,(5,6),0), ("w",2,4,2),
    ("dots",0,(0,1,2),2), ("w",2,3,1), ("w",1,5,3), ("w",1,5,0), ("w",1,8,2), ("w",2,3,0), ("w",0,8,1),
    ("s",0,2), ("dots",1,(0,1,2,3,4,5,6),0), ("w",0,8,3), ("w",0,7,0), ("w",2,4,1), ("dots",1,(7,),0),
    ("kv",1), ("w",1,6,1), ("w",1,5,1), ("w",2,5,2), ("w",2,6,2), ("dots",0,(7,),0), ("kv",0), ("w",2,4,0),
    ("dots",1,(0,1,2,3,4),1), ("dots",0,(3,4),1), ("dots",1,(5,6),1), ("w",2,5,1), ("w",1,7,3), ("w",2,8,2),
    ("w",2,4,3), ("w",2,5,0), ("w",1,8,1), ("dots",1,(7,),1), ("w",2,7,2), ("w",2,6,1), ("q",1), ("w",2,6,0),
    ("dots",0,(5,6),1), ("dots",0,(3,4),2), ("dots",0,(7,),1), ("w",2,6,3), ("dots",0,(5,6),2),
    ("dots",1,(0,1,2,3,4),2), ("dots",1,(5,6),2), ("w",2,8,3), ("w",2,8,1), ("dots",1,(7,),2), ("q",2),
    ("dots",0,(7,),2), ("kvin",), ("att",0,2), ("att",0,1), ("qin",1,0), ("qin",1,1), ("att",1,1),
    ("qin",2,0), ("att",1,2,0), ("qin",2,1), ("att",1,2,1),
)


def kernel(tok, w, kvw, qg_in, kg_in, freq_in, dl_in, out,
           tokb, wbuf, kvbuf, stage, acc, kvacc, kvst, kvin, cosb, sinb, bias, ost, qst, qin, qg, kg, freq, dl,
           send, rw, rt, rs, rkv, rq, loc):
    dp = lax.axis_index("dp")
    hd = lax.axis_index("head")
    x, z = dp // 8, dp % 8
    y, c = hd // 2, hd % 2
    side = x // 2
    xn, xp = x + 1 - 2 * (x % 2), 3 - x
    worker = c == side
    is_v = y // 2
    kv_to = 2 * (y % 2) + side

    def dev(xx, zz, yy, cc):
        return (xx * 8 + zz, yy * 2 + cc)

    near = dev(xn, z, y, c)
    pair = dev(xp, z, y, c)
    up, down = dev(x, (z + 1) % 8, y, c), dev(x, (z + 7) % 8, y, c)
    yup, ydown = dev(x, z, (y + 1) % 4, c), dev(x, z, (y + 3) % 4, c)
    sib = dev(x, z, y, 1 - c)

    small = [pltpu.make_async_copy(a, b, loc.at[4 + n])
             for n, (a, b) in enumerate(((qg_in, qg), (kg_in, kg), (freq_in, freq), (dl_in, dl)))]

    def columns(of_side, g):
        return w.at[:, pl.ds(pl.multiple_of(of_side * 512 + (g - 1) * 256, 256), 256)]

    load_kv = pltpu.make_async_copy(kvw, kvbuf.at[0], loc.at[1])
    load_kv.start()
    for g in (1, 2):
        pltpu.make_async_copy(columns(side, g), wbuf.at[g - 1, 0], loc.at[2]).start()
        pltpu.make_async_copy(columns(1 - side, g), stage.at[g - 1], loc.at[2]).start()
    load_tok = pltpu.make_async_copy(tok, tokb.at[0], loc.at[0])
    load_tok.start()
    for copy in small:
        copy.start()

    barrier = pltpu.get_barrier_semaphore()
    for peer in (near, pair, up, down, yup, ydown, sib):
        pl.semaphore_signal(barrier, inc=1, device_id=peer, device_id_type=MESH)
    src_side = y % 2
    src_x = jnp.where(side == src_side, x, xp)
    kv_self = worker & (kv_to == y)
    for v in (0, 1):
        src_y = 2 * v + y // 2
        @pl.when(jnp.logical_not(kv_self & (is_v == v)))
        def _():
            pl.semaphore_signal(
                barrier, inc=1, device_id=dev(src_x, z, src_y, src_side), device_id_type=MESH)
    extra = jnp.where(worker, jnp.where(kv_to == y, 3, 4), 0)
    pl.semaphore_wait(barrier, 7 + extra)

    def push(src, dst, rsem, to, sid):
        pltpu.make_async_remote_copy(
            src_ref=src, dst_ref=dst, send_sem=send.at[sid], recv_sem=rsem,
            device_id=to, device_id_type=MESH).start()

    def arrive(dst, sem):
        pltpu.make_async_copy(dst, dst, sem).wait()

    def group(g):
        return kvbuf if g == 0 else wbuf.at[g - 1]

    def slot(g, q, xi):
        if q < 7:
            return group(g).at[4 * q + xi]
        return group(g).at[28 + xi, pl.ds(64 * (q - 7), 64), :]

    def half(g, q, xi, h):
        return group(g).at[4 * q + xi, pl.ds(64 * h, 64), :]

    def place(g, q, xi):
        if xi == FAR:
            n, blocks = ((23, 3),) * 3 + ((24, 2),) * 2 + ((25, 2),) * 2 + ((26, 1),) * 2, None
            n, blocks = n[q]
            copies = 2 if blocks == 1 else blocks
        elif xi != PAIR and q >= 7:
            n, blocks, copies = 22, 2, 4
        else:
            n, blocks, copies = (q - 1, q + 6, q + 13)[xi], 1, 1
        return rw.at[g, n], n, blocks, copies

    def rsem_of(g, q, xi):
        return place(g, q, xi)[0]

    def guarded(g, fn):
        if g == 0:
            pl.when(worker)(fn)
        else:
            fn()

    arrivals = {}

    def counted(key, copies):
        arrivals[key] = arrivals.get(key, 0) + 1
        return arrivals[key] == copies

    def wait_w(g, q, xi):
        sem, n, blocks, copies = place(g, q, xi)
        if copies == 1:
            arrive(slot(g, q, xi), sem)
        elif counted((g, n), copies):
            arrive(group(g).at[pl.ds(0, blocks)], sem)

    def ring_start(g, xi):
        def go():
            for d, to in ((1, up), (2, down)):
                push(slot(g, 0, xi), slot(g, d, xi), rsem_of(g, d, xi), to, g)
        guarded(g, go)

    def cross(g, q):
        push(slot(g, q, PAIR), slot(g, q, FAR), rsem_of(g, q, FAR), near, g)

    def start_pair(g):
        if g == 0:
            @pl.when(jnp.logical_not(worker))
            def _():
                push(slot(0, 0, OWN), slot(0, 0, PAIR), rsem_of(0, 0, PAIR), pair, S_HELP)
        else:
            push(stage.at[g - 1], slot(g, 0, PAIR), rsem_of(g, 0, PAIR), pair, g)

    def start_near(g):
        def go():
            push(slot(g, 0, OWN), slot(g, 0, NEAR), rsem_of(g, 0, NEAR), near, g)
        guarded(g, go)

    def cols(head_of):
        return pl.ds(pl.multiple_of(head_of * 512, 512), 512)

    def piece(j, head_of):
        return tokb.at[1, pl.ds(PIECE * j, PIECE), cols(head_of)]

    y_of = (y, (y + 3) % 4, (y + 1) % 4, (y + 2) % 4)

    def tok_pair(s, j):
        of = y_of[s] * 2 + c
        src = tokb.at[0, pl.ds(PIECE * j, PIECE), cols(of)]
        push(src, piece(j, of), rt.at[s, j], pair, S_TOK)

    def tok_arrived(s, j):
        ref = piece(j, y_of[s] * 2 + c)
        arrive(ref, rt.at[s, j])
        if s == 0:
            push(ref, ref, rt.at[1, j], yup, S_TOK)
            push(ref, ref, rt.at[2, j], ydown, S_TOK)
        if s == 1 and j < RELAYED:
            push(ref, ref, rt.at[3, j], yup, S_TOK)
        if s == 2 and RELAYED <= j < 2 * RELAYED:
            push(ref, ref, rt.at[3, j], ydown, S_TOK)

    def quarter(b, head_of):
        return tokb.at[1, pl.ds(128 * b, 128), cols(head_of)]

    def to_sibling(s, b):
        ref = quarter(b, y_of[s] * 2 + c)
        push(ref, ref, rs.at[0], sib, S_TOK)

    def from_sibling(s, b):
        if counted("sibling", 16):
            arrive(tokb.at[1, pl.ds(0, 256), :], rs.at[0])

    def tables(t):
        rank = dp if t == 0 else xp * 8 + z
        row = lax.broadcasted_iota(jnp.int32, (ROWS, HD), 0)
        lane = lax.broadcasted_iota(jnp.int32, (ROWS, HD), 1)
        start = jnp.zeros((ROWS, HD), jnp.int32)
        end = 0
        for d in range(16):
            n = dl[d, rank]
            end = end + n
            start = start + jnp.where(row >= end, n, 0)
        angle = (row - start).astype(F32) * freq[...]
        cosb[t] = jnp.cos(angle)
        s = jnp.sin(angle)
        sinb[t] = jnp.where(lane < 64, -s, s)
        for j in range(4 if t == 0 else 0):
            col = lane + 128 * j
            bias[:, 128 * j:128 * j + 128] = jnp.where((col >= start) & (col <= row), 0.0, -1e30)

    def norm_rope(u, gain, t, by_matrix_unit=False):
        square = u * u
        if by_matrix_unit:
            high = square.astype(BF16)
            low = (square - high.astype(F32)).astype(BF16)
            ms = jnp.dot(jnp.concatenate([high, low], axis=1), jnp.full((2 * HD, HD), 1.0 / HD, BF16),
                         preferred_element_type=F32)
        else:
            ms = jnp.mean(square, axis=-1, keepdims=True)
        n = u * lax.rsqrt(ms + EPS) * gain
        return (n * cosb[t] + pltpu.roll(n, 64, 1) * sinb[t]).astype(BF16)

    def lhs(t, ps):
        parts = []
        for p in ps:
            zz = (z + 8 + (-1 if p % 2 else 1) * ((p + 1) // 2)) % 8
            for xx in (x, xn, xp, 3 - xn):
                f = pl.multiple_of((xx * 8 + zz) * 128, 128)
                parts.append(tokb[t, :, pl.ds(f, 128)])
        return jnp.concatenate(parts, axis=1)

    def dots(t, ps, g):
        def go():
            width = 128 if g == 0 else 256
            b = group(g)[pl.ds(4 * ps[0], 4 * len(ps))].reshape(512 * len(ps), width)
            total = kvacc.at[t] if g == 0 else acc.at[t, g - 1]
            new = jnp.dot(lhs(t, ps), b, preferred_element_type=F32)
            total[...] = new if ps[0] == 0 else total[...] + new
        guarded(g, go)

    def kv_finish(t):
        @pl.when(worker & (is_v == 0))
        def _():
            kvst[t] = norm_rope(kvacc[t], kg[...], t)

        @pl.when(worker & (is_v == 1))
        def _():
            kvst[t] = kvacc[t].astype(BF16)

    def kv_send(t):
        def send_to(xx, core, sid):
            push(kvst.at[t], kvin.at[is_v], rkv.at[0], dev(xx, z, kv_to, core), sid)

        @pl.when(worker)
        def _():
            if t == 1:
                send_to(xp, c, S_KEYS)
                send_to(xp, 1 - c, S_KEYS)
            else:
                send_to(x, 1 - c, S_KEYS)

        if t == 1:
            return
        pl.when(worker & (kv_to != y))(lambda: send_to(x, c, S_BEYOND))

        @pl.when(worker & (kv_to == y))
        def _():
            pltpu.make_async_copy(kvst.at[t], kvin.at[is_v], rkv.at[0]).start()

    def kv_arrived():
        arrive(kvin, rkv.at[0])

    scale = HD ** -0.5 * math.log2(math.e)

    def query(t, g, hh):
        u = acc[t, g - 1, :, 128 * hh:128 * hh + 128]
        return norm_rope(u, qg[...], t, by_matrix_unit=t == 0)

    def send_queries(g):
        for hh in (0, 1):
            n = 2 * (g - 1) + hh
            qst[n] = query(1, g, hh)
            push(qst.at[n], qin.at[n], rq.at[n], pair, S_QUERY)

    def attend(of, g, hh):
        n = 2 * (g - 1) + hh
        q = query(0, g, hh) if of == 0 else qin[n]
        for i in (0, 1):
            m = 256 * (i + 1)
            s = lax.dot_general(q[256 * i:m], kvin[0, :m], (((1,), (1,)), ((), ())),
                                preferred_element_type=F32)
            e = jnp.exp2(s * scale + bias[256 * i:m, :m]).astype(BF16)
            v = jnp.concatenate([kvin[1, :m], jnp.ones((m, HD), BF16)], axis=1)
            o = jnp.dot(e, v, preferred_element_type=F32)
            ost[of, 256 * i:m, 128 * n:128 * n + 128] = (o[:, :HD] / o[:, HD:]).astype(BF16)

    def emit(of, g, hh):
        at = 128 * (2 * (g - 1) + hh)
        first_col = (side if of == 0 else 1 - side) * 512 + at
        pltpu.make_async_copy(ost.at[of, :, pl.ds(at, 128)],
                              out.at[:, pl.ds(pl.multiple_of(first_col, 128), 128)], loc.at[3]).start()

    def weights(g, q, xi):
        def go():
            wait_w(g, q, xi)
            if 0 < q < 7 and xi != FAR:
                d = (q + 1) % 2
                src = slot(g, q, xi) if q < 5 else half(g, q, xi, d)
                on = q + 2
                push(src, slot(g, on, xi), rsem_of(g, on, xi), (up, down)[d], g)
            if xi == PAIR:
                cross(g, q)
        guarded(g, go)

    load_kv.wait()
    arrive(wbuf.at[0, pl.ds(0, 4)], loc.at[2])
    once = set()

    def first(name):
        new = name not in once
        once.add(name)
        return new

    for what, *a in ORDER:
        if what == "tables" and first("small"):
            for copy in small:
                copy.wait()
        if what in ("dots", "tokp", "tokp2") and first("tok"):
            load_tok.wait()
        if what == "near":
            start_near(*a)
        elif what == "pair":
            start_pair(*a)
        elif what == "tokp":
            tok_pair(0, *a)
        elif what == "tokp2":
            tok_pair(3, *a)
        elif what == "src":
            ring_start(*a)
        elif what == "w":
            weights(*a)
        elif what == "t":
            tok_arrived(*a)
        elif what == "sib":
            to_sibling(*a)
        elif what == "s":
            from_sibling(*a)
        elif what == "tables":
            tables(*a)
        elif what == "dots":
            dots(*a)
        elif what == "kv":
            kv_finish(*a)
            kv_send(*a)
        elif what == "kvin":
            kv_arrived()
        elif what == "q":
            send_queries(*a)
        elif what == "qin":
            n = 2 * (a[0] - 1) + a[1]
            arrive(qin.at[n], rq.at[n])
        elif what == "att":
            heads = (0, 1) if len(a) == 2 else a[2:]
            for hh in heads:
                attend(a[0], a[1], hh)
            for hh in heads:
                emit(a[0], a[1], hh)

    for g in (1, 2):
        arrive(group(g).at[pl.ds(0, 31)], send.at[g])
    arrive(tokb.at[1], send.at[S_TOK])
    arrive(qst, send.at[S_QUERY])

    @pl.when(worker)
    def _():
        arrive(kvbuf.at[pl.ds(0, 30)], send.at[S_KV])
        arrive(wbuf.at[0, pl.ds(0, 6)], send.at[S_KEYS])

    @pl.when(worker & (kv_to != y))
    def _():
        arrive(kvst.at[0], send.at[S_BEYOND])

    @pl.when(jnp.logical_not(worker))
    def _():
        arrive(kvbuf.at[0], send.at[S_HELP])

    arrive(ost, loc.at[3])


def shards(tokens, q_weight, kv_weight, q_gain, k_gain, doc_lengths):
    half = np.exp(np.arange(64) * (-2.0 * math.log(THETA) / HD)).astype(np.float32)
    freq = jnp.asarray(np.concatenate([half, half])[None, :])
    any_ = pl.BlockSpec(memory_space=pl.ANY)
    dma = pltpu.SemaphoreType.DMA
    operands = (tokens, q_weight, kv_weight, q_gain[None, :], k_gain[None, :], freq, doc_lengths.T)
    operands = [pltpu.with_memory_space_constraint(a, pltpu.HBM) for a in operands]
    return pl.pallas_call(
        kernel,
        out_shape=jax.ShapeDtypeStruct((ROWS, 1024), BF16),
        in_specs=[any_] * 7,
        out_specs=any_,
        scratch_shapes=[
            pltpu.VMEM((2, ROWS, FEAT), BF16),
            pltpu.VMEM((2, 32, 128, 256), BF16),
            pltpu.VMEM((32, 128, 128), BF16),
            pltpu.VMEM((2, 128, 256), BF16),
            pltpu.VMEM((2, 2, ROWS, 256), F32),
            pltpu.VMEM((2, ROWS, 128), F32),
            pltpu.VMEM((2, ROWS, 128), BF16),
            pltpu.VMEM((2, ROWS, 128), BF16),
            pltpu.VMEM((2, ROWS, HD), F32),
            pltpu.VMEM((2, ROWS, HD), F32),
            pltpu.VMEM((ROWS, ROWS), F32),
            pltpu.VMEM((2, ROWS, 512), BF16),
            pltpu.VMEM((4, ROWS, HD), BF16),
            pltpu.VMEM((4, ROWS, HD), BF16),
            pltpu.VMEM((1, HD), F32),
            pltpu.VMEM((1, HD), F32),
            pltpu.VMEM((1, HD), F32),
            pltpu.SMEM((16, 32), jnp.int32),
            dma((8,)),
            dma((3, 27)),
            dma((4, 8)),
            dma((1,)),
            dma((1,)),
            dma((4,)),
            dma((8,)),
        ],
        compiler_params=pltpu.CompilerParams(
            collective_id=0, has_side_effects=True, vmem_limit_bytes=24 * 2**20),
        cost_estimate=pl.CostEstimate(
            flops=6_000_000_000, bytes_accessed=12 * 2**20, transcendentals=2**21),
    )(*operands)


def solution(mesh):
    placed = (P("dp", None), P("dp", "head"), P("dp", "head"), P(), P(), P())
    return jax.shard_map(
        shards, mesh=mesh, in_specs=placed, out_specs=P("dp", "head"), check_vma=False
    )
```

```python
import functools
import math

import jax
import jax.numpy as jnp
import numpy as np
from jax import lax
from jax.experimental import pallas as pl
from jax.experimental.pallas import tpu as pltpu
from jax.sharding import PartitionSpec as P

HD = 128
ROWS = 512
FEAT = 4096
THETA = 1000000.0
EPS = 1e-06
MESH = pl.DeviceIdType.MESH
F32 = jnp.float32
BF16 = jnp.bfloat16
S_KV, S_HELP, S_TOK, S_KEYS, S_BEYOND, S_QUERY = 0, 3, 4, 5, 6, 7
GROUPS = (0, 1, 2)
OWN, NEAR, PAIR, FAR = 0, 1, 2, 3


PIECE = 64
RELAYED = 2

ORDER = (
    ("w",0,2,3), ("w",2,8,0), ("w",0,5,3), ("w",2,5,3), ("pair",0), ("s",3,2), ("w",1,1,3), ("s",2,3),
    ("near",0), ("pair",1), ("src",2,0), ("near",2), ("s",1,0), ("tables",1), ("pair",2), ("s",1,2),
    ("src",0,0), ("src",1,0), ("w",0,0,2), ("src",0,2), ("w",1,2,3), ("tokp",3), ("tokp",0), ("near",1),
    ("w",0,8,0), ("w",0,2,0), ("w",1,0,2), ("src",1,2), ("w",2,0,2), ("w",0,0,1), ("w",2,7,0), ("src",0,1),
    ("w",2,0,1), ("w",0,1,0), ("tokp",2), ("src",2,2), ("w",1,2,0), ("tokp",1), ("w",2,1,0), ("w",0,0,3),
    ("s",2,0), ("t",0,3), ("s",1,1), ("w",0,1,2), ("tokp",4), ("t",0,0), ("w",0,2,2), ("w",2,2,0),
    ("w",1,1,2), ("w",1,1,0), ("w",1,0,1), ("s",0,0), ("w",1,2,2), ("w",1,3,3), ("tokp",7), ("w",0,3,0),
    ("tokp",6), ("t",0,2), ("w",0,1,1), ("s",0,3), ("t",0,1), ("src",1,1), ("tokp2",6), ("w",1,3,2),
    ("w",0,2,1), ("tokp",5), ("s",3,1), ("w",0,3,2), ("s",2,1), ("w",0,4,2), ("src",2,1), ("t",1,0),
    ("t",0,4), ("tokp2",7), ("t",2,2), ("t",2,3), ("s",3,0), ("w",0,4,0), ("w",1,4,2), ("s",2,2),
    ("w",1,4,0), ("t",1,1), ("w",0,3,1), ("w",2,1,2), ("tokp2",5), ("w",2,0,3), ("w",1,1,1), ("tokp2",4),
    ("w",0,6,2), ("w",0,4,1), ("s",1,3), ("w",2,7,1), ("w",2,3,3), ("w",1,2,1), ("w",0,7,1), ("t",0,6),
    ("sib",0,0), ("w",1,8,0), ("t",0,7), ("w",1,0,3), ("w",2,2,2), ("w",2,7,3), ("w",0,5,2), ("w",1,5,2),
    ("w",1,3,0), ("w",2,2,1), ("t",0,5), ("w",1,8,3), ("sib",1,0), ("tables",0), ("w",2,1,1), ("w",1,7,1),
    ("t",1,6), ("t",1,2), ("s",0,1), ("t",3,3), ("t",3,5), ("w",0,5,0), ("t",3,2), ("s",3,3), ("sib",0,2),
    ("t",1,3), ("t",2,4), ("t",3,0), ("sib",3,1), ("t",2,6), ("w",0,5,1), ("w",2,2,3), ("w",1,6,2),
    ("sib",1,1), ("w",0,8,2), ("t",3,1), ("t",1,4), ("t",2,1), ("w",0,6,1), ("w",0,3,3), ("sib",3,0),
    ("w",0,7,3), ("w",0,1,3), ("sib",0,1), ("t",3,4), ("w",0,6,0), ("sib",3,2), ("w",2,3,2), ("t",2,7),
    ("w",1,6,0), ("w",1,7,0), ("sib",2,3), ("w",2,1,3), ("w",1,3,1), ("t",1,7), ("sib",2,1), ("sib",0,3),
    ("t",3,7), ("t",1,5), ("w",0,7,2), ("t",2,5), ("t",3,6), ("sib",2,2), ("t",2,0), ("w",1,4,1),
    ("w",0,6,3), ("sib",2,0), ("sib",3,3), ("w",0,4,3), ("sib",1,3), ("w",1,7,2), ("sib",1,2), ("w",1,6,3),
    ("w",1,4,3), ("dots",0,(0,1,2),1), ("dots",0,(0,1,2,3,4),0), ("dots",0,(5,6),0), ("w",2,4,2),
    ("dots",0,(0,1,2),2), ("w",2,3,1), ("w",1,5,3), ("w",1,5,0), ("w",1,8,2), ("w",2,3,0), ("w",0,8,1),
    ("s",0,2), ("dots",1,(0,1,2,3,4,5,6),0), ("w",0,8,3), ("w",0,7,0), ("w",2,4,1), ("dots",1,(7,),0),
    ("kv",1), ("w",1,6,1), ("w",1,5,1), ("w",2,5,2), ("w",2,6,2), ("dots",0,(7,),0), ("kv",0), ("w",2,4,0),
    ("dots",1,(0,1,2,3,4),1), ("dots",1,(5,6),1), ("w",2,5,1), ("w",1,7,3), ("w",2,4,3), ("w",2,5,0),
    ("w",1,8,1), ("dots",1,(7,),1), ("w",2,7,2), ("w",2,6,1), ("q",1), ("w",2,8,2), ("dots",0,(3,4),1),
    ("w",2,6,0), ("dots",0,(3,4),2), ("w",2,6,3), ("dots",1,(0,1,2,3,4),2), ("dots",1,(5,6),2), ("w",2,8,3),
    ("w",2,8,1), ("dots",1,(7,),2), ("q",2), ("dots",0,(5,6),2), ("dots",0,(5,6),1), ("dots",0,(7,),1),
    ("dots",0,(7,),2), ("kvin",), ("att",0,2), ("att",0,1), ("qin",1,0), ("qin",1,1), ("att",1,1),
    ("qin",2,0), ("att",1,2,0), ("qin",2,1), ("att",1,2,1),
)


def kernel(tok, w, kvw, qg_in, kg_in, freq_in, dl_in, out,
           tokb, wbuf, kvbuf, stage, acc, kvacc, kvst, kvin, cosb, sinb, bias, ost, qst, qin, qg, kg, freq, dl,
           send, rw, rt, rs, rkv, rq, loc):
    dp = lax.axis_index("dp")
    hd = lax.axis_index("head")
    x, z = dp // 8, dp % 8
    y, c = hd // 2, hd % 2
    side = x // 2
    xn, xp = x + 1 - 2 * (x % 2), 3 - x
    worker = c == side
    is_v = y // 2
    kv_to = 2 * (y % 2) + side

    def dev(xx, zz, yy, cc):
        return (xx * 8 + zz, yy * 2 + cc)

    near = dev(xn, z, y, c)
    pair = dev(xp, z, y, c)
    up, down = dev(x, (z + 1) % 8, y, c), dev(x, (z + 7) % 8, y, c)
    yup, ydown = dev(x, z, (y + 1) % 4, c), dev(x, z, (y + 3) % 4, c)
    sib = dev(x, z, y, 1 - c)

    small = [pltpu.make_async_copy(a, b, loc.at[4 + n])
             for n, (a, b) in enumerate(((qg_in, qg), (kg_in, kg), (freq_in, freq), (dl_in, dl)))]

    def columns(of_side, g):
        return w.at[:, pl.ds(pl.multiple_of(of_side * 512 + (g - 1) * 256, 256), 256)]

    load_kv = pltpu.make_async_copy(kvw, kvbuf.at[0], loc.at[1])
    load_kv.start()
    for g in (1, 2):
        pltpu.make_async_copy(columns(side, g), wbuf.at[g - 1, 0], loc.at[2]).start()
        pltpu.make_async_copy(columns(1 - side, g), stage.at[g - 1], loc.at[2]).start()
    load_tok = pltpu.make_async_copy(tok, tokb.at[0], loc.at[0])
    load_tok.start()
    for copy in small:
        copy.start()

    barrier = pltpu.get_barrier_semaphore()
    for peer in (near, pair, up, down, yup, ydown, sib):
        pl.semaphore_signal(barrier, inc=1, device_id=peer, device_id_type=MESH)
    src_side = y % 2
    src_x = jnp.where(side == src_side, x, xp)
    kv_self = worker & (kv_to == y)
    for v in (0, 1):
        src_y = 2 * v + y // 2
        @pl.when(jnp.logical_not(kv_self & (is_v == v)))
        def _():
            pl.semaphore_signal(
                barrier, inc=1, device_id=dev(src_x, z, src_y, src_side), device_id_type=MESH)
    extra = jnp.where(worker, jnp.where(kv_to == y, 3, 4), 0)
    pl.semaphore_wait(barrier, 7 + extra)

    def push(src, dst, rsem, to, sid):
        pltpu.make_async_remote_copy(
            src_ref=src, dst_ref=dst, send_sem=send.at[sid], recv_sem=rsem,
            device_id=to, device_id_type=MESH).start()

    def arrive(dst, sem):
        pltpu.make_async_copy(dst, dst, sem).wait()

    def group(g):
        return kvbuf if g == 0 else wbuf.at[g - 1]

    def slot(g, q, xi):
        if q < 7:
            return group(g).at[4 * q + xi]
        return group(g).at[28 + xi, pl.ds(64 * (q - 7), 64), :]

    def half(g, q, xi, h):
        return group(g).at[4 * q + xi, pl.ds(64 * h, 64), :]

    def place(g, q, xi):
        if xi == FAR:
            n, blocks = ((23, 3),) * 3 + ((24, 2),) * 2 + ((25, 2),) * 2 + ((26, 1),) * 2, None
            n, blocks = n[q]
            copies = 2 if blocks == 1 else blocks
        elif xi != PAIR and q >= 7:
            n, blocks, copies = 22, 2, 4
        else:
            n, blocks, copies = (q - 1, q + 6, q + 13)[xi], 1, 1
        return rw.at[g, n], n, blocks, copies

    def rsem_of(g, q, xi):
        return place(g, q, xi)[0]

    def guarded(g, fn):
        if g == 0:
            pl.when(worker)(fn)
        else:
            fn()

    arrivals = {}

    def counted(key, copies):
        arrivals[key] = arrivals.get(key, 0) + 1
        return arrivals[key] == copies

    def wait_w(g, q, xi):
        sem, n, blocks, copies = place(g, q, xi)
        if copies == 1:
            arrive(slot(g, q, xi), sem)
        elif counted((g, n), copies):
            arrive(group(g).at[pl.ds(0, blocks)], sem)

    def ring_start(g, xi):
        def go():
            for d, to in ((1, up), (2, down)):
                push(slot(g, 0, xi), slot(g, d, xi), rsem_of(g, d, xi), to, g)
        guarded(g, go)

    def cross(g, q):
        push(slot(g, q, PAIR), slot(g, q, FAR), rsem_of(g, q, FAR), near, g)

    def start_pair(g):
        if g == 0:
            @pl.when(jnp.logical_not(worker))
            def _():
                push(slot(0, 0, OWN), slot(0, 0, PAIR), rsem_of(0, 0, PAIR), pair, S_HELP)
        else:
            push(stage.at[g - 1], slot(g, 0, PAIR), rsem_of(g, 0, PAIR), pair, g)

    def start_near(g):
        def go():
            push(slot(g, 0, OWN), slot(g, 0, NEAR), rsem_of(g, 0, NEAR), near, g)
        guarded(g, go)

    def cols(head_of):
        return pl.ds(pl.multiple_of(head_of * 512, 512), 512)

    def piece(j, head_of):
        return tokb.at[1, pl.ds(PIECE * j, PIECE), cols(head_of)]

    y_of = (y, (y + 3) % 4, (y + 1) % 4, (y + 2) % 4)

    def tok_pair(s, j):
        of = y_of[s] * 2 + c
        src = tokb.at[0, pl.ds(PIECE * j, PIECE), cols(of)]
        push(src, piece(j, of), rt.at[s, j], pair, S_TOK)

    def tok_arrived(s, j):
        ref = piece(j, y_of[s] * 2 + c)
        arrive(ref, rt.at[s, j])
        if s == 0:
            push(ref, ref, rt.at[1, j], yup, S_TOK)
            push(ref, ref, rt.at[2, j], ydown, S_TOK)
        if s == 1 and j < RELAYED:
            push(ref, ref, rt.at[3, j], yup, S_TOK)
        if s == 2 and RELAYED <= j < 2 * RELAYED:
            push(ref, ref, rt.at[3, j], ydown, S_TOK)

    def quarter(b, head_of):
        return tokb.at[1, pl.ds(128 * b, 128), cols(head_of)]

    def to_sibling(s, b):
        ref = quarter(b, y_of[s] * 2 + c)
        push(ref, ref, rs.at[0], sib, S_TOK)

    def from_sibling(s, b):
        if counted("sibling", 16):
            arrive(tokb.at[1, pl.ds(0, 256), :], rs.at[0])

    def tables(t):
        rank = dp if t == 0 else xp * 8 + z
        row = lax.broadcasted_iota(jnp.int32, (ROWS, HD), 0)
        lane = lax.broadcasted_iota(jnp.int32, (ROWS, HD), 1)
        start = jnp.zeros((ROWS, HD), jnp.int32)
        end = 0
        for d in range(16):
            n = dl[d, rank]
            end = end + n
            start = start + jnp.where(row >= end, n, 0)
        angle = (row - start).astype(F32) * freq[...]
        cosb[t] = jnp.cos(angle)
        s = jnp.sin(angle)
        sinb[t] = jnp.where(lane < 64, -s, s)
        for j in range(4 if t == 0 else 0):
            col = lane + 128 * j
            bias[:, 128 * j:128 * j + 128] = jnp.where((col >= start) & (col <= row), 0.0, -1e30)

    def norm_rope(u, gain, t, by_matrix_unit=False):
        square = u * u
        if by_matrix_unit:
            high = square.astype(BF16)
            low = (square - high.astype(F32)).astype(BF16)
            ms = jnp.dot(jnp.concatenate([high, low], axis=1), jnp.full((2 * HD, HD), 1.0 / HD, BF16),
                         preferred_element_type=F32)
        else:
            ms = jnp.mean(square, axis=-1, keepdims=True)
        n = u * lax.rsqrt(ms + EPS) * gain
        return (n * cosb[t] + pltpu.roll(n, 64, 1) * sinb[t]).astype(BF16)

    def lhs(t, ps):
        parts = []
        for p in ps:
            zz = (z + 8 + (-1 if p % 2 else 1) * ((p + 1) // 2)) % 8
            for xx in (x, xn, xp, 3 - xn):
                f = pl.multiple_of((xx * 8 + zz) * 128, 128)
                parts.append(tokb[t, :, pl.ds(f, 128)])
        return jnp.concatenate(parts, axis=1)

    def dots(t, ps, g):
        def go():
            width = 128 if g == 0 else 256
            b = group(g)[pl.ds(4 * ps[0], 4 * len(ps))].reshape(512 * len(ps), width)
            total = kvacc.at[t] if g == 0 else acc.at[t, g - 1]
            new = jnp.dot(lhs(t, ps), b, preferred_element_type=F32)
            total[...] = new if ps[0] == 0 else total[...] + new
        guarded(g, go)

    def kv_finish(t):
        @pl.when(worker & (is_v == 0))
        def _():
            kvst[t] = norm_rope(kvacc[t], kg[...], t)

        @pl.when(worker & (is_v == 1))
        def _():
            kvst[t] = kvacc[t].astype(BF16)

    def kv_send(t):
        def send_to(xx, core, sid):
            push(kvst.at[t], kvin.at[is_v], rkv.at[0], dev(xx, z, kv_to, core), sid)

        @pl.when(worker)
        def _():
            if t == 1:
                send_to(xp, c, S_KEYS)
                send_to(xp, 1 - c, S_KEYS)
            else:
                send_to(x, 1 - c, S_KEYS)

        if t == 1:
            return
        pl.when(worker & (kv_to != y))(lambda: send_to(x, c, S_BEYOND))

        @pl.when(worker & (kv_to == y))
        def _():
            pltpu.make_async_copy(kvst.at[t], kvin.at[is_v], rkv.at[0]).start()

    def kv_arrived():
        arrive(kvin, rkv.at[0])

    scale = HD ** -0.5 * math.log2(math.e)

    def query(t, g, hh):
        u = acc[t, g - 1, :, 128 * hh:128 * hh + 128]
        return norm_rope(u, qg[...], t, by_matrix_unit=t == 0)

    def send_queries(g):
        for hh in (0, 1):
            n = 2 * (g - 1) + hh
            qst[n] = query(1, g, hh)
            push(qst.at[n], qin.at[n], rq.at[n], pair, S_QUERY)

    def attend(of, g, hh):
        n = 2 * (g - 1) + hh
        q = query(0, g, hh) if of == 0 else qin[n]
        for i in (0, 1):
            m = 256 * (i + 1)
            s = lax.dot_general(q[256 * i:m], kvin[0, :m], (((1,), (1,)), ((), ())),
                                preferred_element_type=F32)
            e = jnp.exp2(s * scale + bias[256 * i:m, :m]).astype(BF16)
            v = jnp.concatenate([kvin[1, :m], jnp.ones((m, HD), BF16)], axis=1)
            o = jnp.dot(e, v, preferred_element_type=F32)
            ost[of, 256 * i:m, 128 * n:128 * n + 128] = (o[:, :HD] / o[:, HD:]).astype(BF16)

    def emit(of, g, hh):
        at = 128 * (2 * (g - 1) + hh)
        first_col = (side if of == 0 else 1 - side) * 512 + at
        pltpu.make_async_copy(ost.at[of, :, pl.ds(at, 128)],
                              out.at[:, pl.ds(pl.multiple_of(first_col, 128), 128)], loc.at[3]).start()

    def weights(g, q, xi):
        def go():
            wait_w(g, q, xi)
            if 0 < q < 7 and xi != FAR:
                d = (q + 1) % 2
                src = slot(g, q, xi) if q < 5 else half(g, q, xi, d)
                on = q + 2
                push(src, slot(g, on, xi), rsem_of(g, on, xi), (up, down)[d], g)
            if xi == PAIR:
                cross(g, q)
        guarded(g, go)

    load_kv.wait()
    arrive(wbuf.at[0, pl.ds(0, 4)], loc.at[2])
    once = set()

    def first(name):
        new = name not in once
        once.add(name)
        return new

    for what, *a in ORDER:
        if what == "tables" and first("small"):
            for copy in small:
                copy.wait()
        if what in ("dots", "tokp", "tokp2") and first("tok"):
            load_tok.wait()
        if what == "near":
            start_near(*a)
        elif what == "pair":
            start_pair(*a)
        elif what == "tokp":
            tok_pair(0, *a)
        elif what == "tokp2":
            tok_pair(3, *a)
        elif what == "src":
            ring_start(*a)
        elif what == "w":
            weights(*a)
        elif what == "t":
            tok_arrived(*a)
        elif what == "sib":
            to_sibling(*a)
        elif what == "s":
            from_sibling(*a)
        elif what == "tables":
            tables(*a)
        elif what == "dots":
            dots(*a)
        elif what == "kv":
            kv_finish(*a)
            kv_send(*a)
        elif what == "kvin":
            kv_arrived()
        elif what == "q":
            send_queries(*a)
        elif what == "qin":
            n = 2 * (a[0] - 1) + a[1]
            arrive(qin.at[n], rq.at[n])
        elif what == "att":
            heads = (0, 1) if len(a) == 2 else a[2:]
            for hh in heads:
                attend(a[0], a[1], hh)
            for hh in heads:
                emit(a[0], a[1], hh)

    for g in (1, 2):
        arrive(group(g).at[pl.ds(0, 31)], send.at[g])
    arrive(tokb.at[1], send.at[S_TOK])
    arrive(qst, send.at[S_QUERY])

    @pl.when(worker)
    def _():
        arrive(kvbuf.at[pl.ds(0, 30)], send.at[S_KV])
        arrive(wbuf.at[0, pl.ds(0, 6)], send.at[S_KEYS])

    @pl.when(worker & (kv_to != y))
    def _():
        arrive(kvst.at[0], send.at[S_BEYOND])

    @pl.when(jnp.logical_not(worker))
    def _():
        arrive(kvbuf.at[0], send.at[S_HELP])

    arrive(ost, loc.at[3])


def shards(tokens, q_weight, kv_weight, q_gain, k_gain, doc_lengths):
    half = np.exp(np.arange(64) * (-2.0 * math.log(THETA) / HD)).astype(np.float32)
    freq = jnp.asarray(np.concatenate([half, half])[None, :])
    any_ = pl.BlockSpec(memory_space=pl.ANY)
    dma = pltpu.SemaphoreType.DMA
    operands = (tokens, q_weight, kv_weight, q_gain[None, :], k_gain[None, :], freq, doc_lengths.T)
    operands = [pltpu.with_memory_space_constraint(a, pltpu.HBM) for a in operands]
    return pl.pallas_call(
        kernel,
        out_shape=jax.ShapeDtypeStruct((ROWS, 1024), BF16),
        in_specs=[any_] * 7,
        out_specs=any_,
        scratch_shapes=[
            pltpu.VMEM((2, ROWS, FEAT), BF16),
            pltpu.VMEM((2, 32, 128, 256), BF16),
            pltpu.VMEM((32, 128, 128), BF16),
            pltpu.VMEM((2, 128, 256), BF16),
            pltpu.VMEM((2, 2, ROWS, 256), F32),
            pltpu.VMEM((2, ROWS, 128), F32),
            pltpu.VMEM((2, ROWS, 128), BF16),
            pltpu.VMEM((2, ROWS, 128), BF16),
            pltpu.VMEM((2, ROWS, HD), F32),
            pltpu.VMEM((2, ROWS, HD), F32),
            pltpu.VMEM((ROWS, ROWS), F32),
            pltpu.VMEM((2, ROWS, 512), BF16),
            pltpu.VMEM((4, ROWS, HD), BF16),
            pltpu.VMEM((4, ROWS, HD), BF16),
            pltpu.VMEM((1, HD), F32),
            pltpu.VMEM((1, HD), F32),
            pltpu.VMEM((1, HD), F32),
            pltpu.SMEM((16, 32), jnp.int32),
            dma((8,)),
            dma((3, 27)),
            dma((4, 8)),
            dma((1,)),
            dma((1,)),
            dma((4,)),
            dma((8,)),
        ],
        compiler_params=pltpu.CompilerParams(
            collective_id=0, has_side_effects=True, vmem_limit_bytes=24 * 2**20),
        cost_estimate=pl.CostEstimate(
            flops=6_000_000_000, bytes_accessed=12 * 2**20, transcendentals=2**21),
    )(*operands)


def solution(mesh):
    placed = (P("dp", None), P("dp", "head"), P("dp", "head"), P(), P(), P())
    return jax.shard_map(
        shards, mesh=mesh, in_specs=placed, out_specs=P("dp", "head"), check_vma=False
    )
```

```python
import functools
import math

import jax
import jax.numpy as jnp
import numpy as np
from jax import lax
from jax.experimental import pallas as pl
from jax.experimental.pallas import tpu as pltpu
from jax.sharding import PartitionSpec as P

HD = 128
ROWS = 512
FEAT = 4096
THETA = 1000000.0
EPS = 1e-06
MESH = pl.DeviceIdType.MESH
F32 = jnp.float32
BF16 = jnp.bfloat16
S_KV, S_HELP, S_TOK, S_KEYS, S_BEYOND, S_QUERY = 0, 3, 4, 5, 6, 7
GROUPS = (0, 1, 2)
OWN, NEAR, PAIR, FAR = 0, 1, 2, 3


PIECE = 64
RELAYED = 2

ORDER = (
    ("w",0,2,3), ("w",2,8,0), ("w",0,5,3), ("w",2,5,3), ("pair",0), ("s",3,2), ("w",1,1,3), ("s",2,3),
    ("near",0), ("pair",1), ("src",2,0), ("near",2), ("s",1,0), ("tables",1), ("pair",2), ("s",1,2),
    ("src",0,0), ("src",1,0), ("w",0,0,2), ("src",0,2), ("w",1,2,3), ("tokp",3), ("tokp",0), ("near",1),
    ("w",0,8,0), ("w",0,2,0), ("w",1,0,2), ("src",1,2), ("w",2,0,2), ("w",0,0,1), ("w",2,7,0), ("src",0,1),
    ("w",2,0,1), ("w",0,1,0), ("tokp",2), ("src",2,2), ("w",1,2,0), ("tokp",1), ("w",2,1,0), ("w",0,0,3),
    ("s",2,0), ("t",0,3), ("s",1,1), ("w",0,1,2), ("tokp",4), ("t",0,0), ("w",0,2,2), ("w",2,2,0),
    ("w",1,1,2), ("w",1,1,0), ("w",1,0,1), ("s",0,0), ("w",1,2,2), ("w",1,3,3), ("tokp",7), ("w",0,3,0),
    ("tokp",6), ("t",0,2), ("w",0,1,1), ("s",0,3), ("t",0,1), ("src",1,1), ("tokp2",6), ("w",1,3,2),
    ("w",0,2,1), ("tokp",5), ("s",3,1), ("w",0,3,2), ("s",2,1), ("w",0,4,2), ("src",2,1), ("t",1,0),
    ("t",0,4), ("tokp2",7), ("t",2,2), ("t",2,3), ("s",3,0), ("w",0,4,0), ("w",1,4,2), ("s",2,2),
    ("w",1,4,0), ("t",1,1), ("w",0,3,1), ("w",2,1,2), ("tokp2",5), ("w",2,0,3), ("w",1,1,1), ("tokp2",4),
    ("w",0,6,2), ("w",0,4,1), ("s",1,3), ("w",2,7,1), ("w",2,3,3), ("w",1,2,1), ("w",0,7,1), ("t",0,6),
    ("sib",0,0), ("w",1,8,0), ("t",0,7), ("w",1,0,3), ("w",2,2,2), ("w",2,7,3), ("w",0,5,2), ("w",1,5,2),
    ("w",1,3,0), ("w",2,2,1), ("t",0,5), ("w",1,8,3), ("sib",1,0), ("tables",0), ("w",2,1,1), ("w",1,7,1),
    ("t",1,6), ("t",1,2), ("s",0,1), ("t",3,3), ("t",3,5), ("w",0,5,0), ("t",3,2), ("s",3,3), ("sib",0,2),
    ("t",1,3), ("t",2,4), ("t",3,0), ("sib",3,1), ("t",2,6), ("w",0,5,1), ("w",2,2,3), ("w",1,6,2),
    ("sib",1,1), ("w",0,8,2), ("t",3,1), ("t",1,4), ("t",2,1), ("w",0,6,1), ("w",0,3,3), ("sib",3,0),
    ("w",0,7,3), ("w",0,1,3), ("sib",0,1), ("t",3,4), ("w",0,6,0), ("sib",3,2), ("w",2,3,2), ("t",2,7),
    ("w",1,6,0), ("w",1,7,0), ("sib",2,3), ("w",2,1,3), ("w",1,3,1), ("t",1,7), ("sib",2,1), ("sib",0,3),
    ("t",3,7), ("t",1,5), ("w",0,7,2), ("t",2,5), ("t",3,6), ("sib",2,2), ("t",2,0), ("w",1,4,1),
    ("w",0,6,3), ("sib",2,0), ("sib",3,3), ("w",0,4,3), ("sib",1,3), ("w",1,7,2), ("sib",1,2), ("w",1,6,3),
    ("w",1,4,3), ("dots",0,(0,1,2),1), ("dots",0,(0,1,2,3,4),0), ("dots",0,(5,6),0), ("w",2,4,2),
    ("dots",0,(0,1,2),2), ("w",2,3,1), ("w",1,5,3), ("w",1,5,0), ("w",1,8,2), ("w",2,3,0), ("w",0,8,1),
    ("s",0,2), ("dots",1,(0,1,2,3,4,5,6),0), ("w",0,8,3), ("w",0,7,0), ("w",2,4,1), ("dots",1,(7,),0),
    ("kv",1), ("w",1,6,1), ("w",1,5,1), ("w",2,5,2), ("w",2,6,2), ("dots",0,(7,),0), ("kv",0), ("w",2,4,0),
    ("dots",1,(0,1,2,3,4),1), ("dots",0,(3,4),1), ("dots",1,(5,6),1), ("w",2,5,1), ("w",1,7,3), ("w",2,8,2),
    ("w",2,4,3), ("w",2,5,0), ("w",1,8,1), ("dots",1,(7,),1), ("w",2,7,2), ("w",2,6,1), ("q",1), ("w",2,6,0),
    ("dots",0,(5,6),1), ("dots",0,(3,4),2), ("dots",0,(7,),1), ("w",2,6,3), ("dots",0,(5,6),2),
    ("dots",1,(0,1,2,3,4),2), ("dots",1,(5,6),2), ("w",2,8,3), ("w",2,8,1), ("dots",1,(7,),2), ("q",2),
    ("dots",0,(7,),2), ("kvin",), ("att",0,2), ("att",0,1), ("qin",1,0), ("qin",1,1), ("att",1,1),
    ("qin",2,0), ("att",1,2,0), ("qin",2,1), ("att",1,2,1),
)


def kernel(tok, w, kvw, qg_in, kg_in, freq_in, dl_in, out,
           tokb, wbuf, kvbuf, stage, acc, kvacc, kvst, kvin, cosb, sinb, bias, ost, qst, qin, own, qg, kg, freq, dl,
           send, rw, rt, rs, rkv, rq, loc):
    dp = lax.axis_index("dp")
    hd = lax.axis_index("head")
    x, z = dp // 8, dp % 8
    y, c = hd // 2, hd % 2
    side = x // 2
    xn, xp = x + 1 - 2 * (x % 2), 3 - x
    worker = c == side
    is_v = y // 2
    kv_to = 2 * (y % 2) + side

    def dev(xx, zz, yy, cc):
        return (xx * 8 + zz, yy * 2 + cc)

    near = dev(xn, z, y, c)
    pair = dev(xp, z, y, c)
    up, down = dev(x, (z + 1) % 8, y, c), dev(x, (z + 7) % 8, y, c)
    yup, ydown = dev(x, z, (y + 1) % 4, c), dev(x, z, (y + 3) % 4, c)
    sib = dev(x, z, y, 1 - c)

    small = [pltpu.make_async_copy(a, b, loc.at[4 + n])
             for n, (a, b) in enumerate(((qg_in, qg), (kg_in, kg), (freq_in, freq), (dl_in, dl)))]

    def columns(of_side, g):
        return w.at[:, pl.ds(pl.multiple_of(of_side * 512 + (g - 1) * 256, 256), 256)]

    load_kv = pltpu.make_async_copy(kvw, kvbuf.at[0], loc.at[1])
    load_kv.start()
    for g in (1, 2):
        pltpu.make_async_copy(columns(side, g), wbuf.at[g - 1, 0], loc.at[2]).start()
        pltpu.make_async_copy(columns(1 - side, g), stage.at[g - 1], loc.at[2]).start()
    load_tok = pltpu.make_async_copy(tok, tokb.at[0], loc.at[0])
    load_tok.start()
    for copy in small:
        copy.start()

    barrier = pltpu.get_barrier_semaphore()
    for peer in (near, pair, up, down, yup, ydown, sib):
        pl.semaphore_signal(barrier, inc=1, device_id=peer, device_id_type=MESH)
    src_side = y % 2
    src_x = jnp.where(side == src_side, x, xp)
    kv_self = worker & (kv_to == y)
    for v in (0, 1):
        src_y = 2 * v + y // 2
        @pl.when(jnp.logical_not(kv_self & (is_v == v)))
        def _():
            pl.semaphore_signal(
                barrier, inc=1, device_id=dev(src_x, z, src_y, src_side), device_id_type=MESH)
    extra = jnp.where(worker, jnp.where(kv_to == y, 3, 4), 0)
    pl.semaphore_wait(barrier, 7 + extra)

    def push(src, dst, rsem, to, sid):
        pltpu.make_async_remote_copy(
            src_ref=src, dst_ref=dst, send_sem=send.at[sid], recv_sem=rsem,
            device_id=to, device_id_type=MESH).start()

    def arrive(dst, sem):
        pltpu.make_async_copy(dst, dst, sem).wait()

    def group(g):
        return kvbuf if g == 0 else wbuf.at[g - 1]

    def slot(g, q, xi):
        if q < 7:
            return group(g).at[4 * q + xi]
        return group(g).at[28 + xi, pl.ds(64 * (q - 7), 64), :]

    def half(g, q, xi, h):
        return group(g).at[4 * q + xi, pl.ds(64 * h, 64), :]

    def place(g, q, xi):
        if xi == FAR:
            n, blocks = ((23, 3),) * 3 + ((24, 2),) * 2 + ((25, 2),) * 2 + ((26, 1),) * 2, None
            n, blocks = n[q]
            copies = 2 if blocks == 1 else blocks
        elif xi != PAIR and q >= 7:
            n, blocks, copies = 22, 2, 4
        else:
            n, blocks, copies = (q - 1, q + 6, q + 13)[xi], 1, 1
        return rw.at[g, n], n, blocks, copies

    def rsem_of(g, q, xi):
        return place(g, q, xi)[0]

    def guarded(g, fn):
        if g == 0:
            pl.when(worker)(fn)
        else:
            fn()

    arrivals = {}

    def counted(key, copies):
        arrivals[key] = arrivals.get(key, 0) + 1
        return arrivals[key] == copies

    def wait_w(g, q, xi):
        sem, n, blocks, copies = place(g, q, xi)
        if copies == 1:
            arrive(slot(g, q, xi), sem)
        elif counted((g, n), copies):
            arrive(group(g).at[pl.ds(0, blocks)], sem)

    def ring_start(g, xi):
        def go():
            for d, to in ((1, up), (2, down)):
                push(slot(g, 0, xi), slot(g, d, xi), rsem_of(g, d, xi), to, g)
        guarded(g, go)

    def cross(g, q):
        push(slot(g, q, PAIR), slot(g, q, FAR), rsem_of(g, q, FAR), near, g)

    def start_pair(g):
        if g == 0:
            @pl.when(jnp.logical_not(worker))
            def _():
                push(slot(0, 0, OWN), slot(0, 0, PAIR), rsem_of(0, 0, PAIR), pair, S_HELP)
        else:
            push(stage.at[g - 1], slot(g, 0, PAIR), rsem_of(g, 0, PAIR), pair, g)

    def start_near(g):
        def go():
            push(slot(g, 0, OWN), slot(g, 0, NEAR), rsem_of(g, 0, NEAR), near, g)
        guarded(g, go)

    def cols(head_of):
        return pl.ds(pl.multiple_of(head_of * 512, 512), 512)

    def piece(j, head_of):
        return tokb.at[1, pl.ds(PIECE * j, PIECE), cols(head_of)]

    y_of = (y, (y + 3) % 4, (y + 1) % 4, (y + 2) % 4)

    def tok_pair(s, j):
        of = y_of[s] * 2 + c
        src = tokb.at[0, pl.ds(PIECE * j, PIECE), cols(of)]
        push(src, piece(j, of), rt.at[s, j], pair, S_TOK)

    def tok_arrived(s, j):
        ref = piece(j, y_of[s] * 2 + c)
        arrive(ref, rt.at[s, j])
        if s == 0:
            push(ref, ref, rt.at[1, j], yup, S_TOK)
            push(ref, ref, rt.at[2, j], ydown, S_TOK)
        if s == 1 and j < RELAYED:
            push(ref, ref, rt.at[3, j], yup, S_TOK)
        if s == 2 and RELAYED <= j < 2 * RELAYED:
            push(ref, ref, rt.at[3, j], ydown, S_TOK)

    def quarter(b, head_of):
        return tokb.at[1, pl.ds(128 * b, 128), cols(head_of)]

    def to_sibling(s, b):
        ref = quarter(b, y_of[s] * 2 + c)
        push(ref, ref, rs.at[0], sib, S_TOK)

    def from_sibling(s, b):
        if counted("sibling", 16):
            arrive(tokb.at[1, pl.ds(0, 256), :], rs.at[0])

    def tables(t):
        rank = dp if t == 0 else xp * 8 + z
        row = lax.broadcasted_iota(jnp.int32, (ROWS, HD), 0)
        lane = lax.broadcasted_iota(jnp.int32, (ROWS, HD), 1)
        start = jnp.zeros((ROWS, HD), jnp.int32)
        end = 0
        for d in range(16):
            n = dl[d, rank]
            end = end + n
            start = start + jnp.where(row >= end, n, 0)
        angle = (row - start).astype(F32) * freq[...]
        cosb[t] = jnp.cos(angle)
        s = jnp.sin(angle)
        sinb[t] = jnp.where(lane < 64, -s, s)
        for j in range(4 if t == 0 else 0):
            col = lane + 128 * j
            bias[:, 128 * j:128 * j + 128] = jnp.where((col >= start) & (col <= row), 0.0, -1e30)

    def norm_rope(u, gain, t, by_matrix_unit=False):
        square = u * u
        if by_matrix_unit:
            high = square.astype(BF16)
            low = (square - high.astype(F32)).astype(BF16)
            ms = jnp.dot(jnp.concatenate([high, low], axis=1), jnp.full((2 * HD, HD), 1.0 / HD, BF16),
                         preferred_element_type=F32)
        else:
            ms = jnp.mean(square, axis=-1, keepdims=True)
        n = u * lax.rsqrt(ms + EPS) * gain
        return (n * cosb[t] + pltpu.roll(n, 64, 1) * sinb[t]).astype(BF16)

    def lhs(t, ps):
        parts = []
        for p in ps:
            zz = (z + 8 + (-1 if p % 2 else 1) * ((p + 1) // 2)) % 8
            for xx in (x, xn, xp, 3 - xn):
                f = pl.multiple_of((xx * 8 + zz) * 128, 128)
                parts.append(tokb[t, :, pl.ds(f, 128)])
        return jnp.concatenate(parts, axis=1)

    def dots(t, ps, g):
        def go():
            width = 128 if g == 0 else 256
            b = group(g)[pl.ds(4 * ps[0], 4 * len(ps))].reshape(512 * len(ps), width)
            total = kvacc.at[t] if g == 0 else acc.at[t, g - 1]
            new = jnp.dot(lhs(t, ps), b, preferred_element_type=F32)
            total[...] = new if ps[0] == 0 else total[...] + new
        guarded(g, go)

    def kv_finish(t):
        @pl.when(worker & (is_v == 0))
        def _():
            kvst[t] = norm_rope(kvacc[t], kg[...], t)

        @pl.when(worker & (is_v == 1))
        def _():
            kvst[t] = kvacc[t].astype(BF16)

    def kv_send(t):
        def send_to(xx, core, sid):
            push(kvst.at[t], kvin.at[is_v], rkv.at[0], dev(xx, z, kv_to, core), sid)

        @pl.when(worker)
        def _():
            if t == 1:
                send_to(xp, c, S_KEYS)
                send_to(xp, 1 - c, S_KEYS)
            else:
                send_to(x, 1 - c, S_KEYS)

        if t == 1:
            return
        pl.when(worker & (kv_to != y))(lambda: send_to(x, c, S_BEYOND))

        @pl.when(worker & (kv_to == y))
        def _():
            pltpu.make_async_copy(kvst.at[t], kvin.at[is_v], rkv.at[0]).start()

    def kv_arrived():
        arrive(kvin, rkv.at[0])

    scale = HD ** -0.5 * math.log2(math.e)

    def query(t, g, hh):
        u = acc[t, g - 1, :, 128 * hh:128 * hh + 128]
        return norm_rope(u, qg[...], t, by_matrix_unit=False)

    def send_queries(g):
        for hh in (0, 1):
            n = 2 * (g - 1) + hh
            qst[n] = query(1, g, hh)
            push(qst.at[n], qin.at[n], rq.at[n], pair, S_QUERY)

    def attend(of, g, hh):
        n = 2 * (g - 1) + hh
        q = own[n] if of == 0 else qin[n]
        for i in (0, 1):
            m = 256 * (i + 1)
            s = lax.dot_general(q[256 * i:m], kvin[0, :m], (((1,), (1,)), ((), ())),
                                preferred_element_type=F32)
            e = jnp.exp2(s * scale + bias[256 * i:m, :m]).astype(BF16)
            v = jnp.concatenate([kvin[1, :m], jnp.ones((m, HD), BF16)], axis=1)
            o = jnp.dot(e, v, preferred_element_type=F32)
            ost[of, 256 * i:m, 128 * n:128 * n + 128] = (o[:, :HD] / o[:, HD:]).astype(BF16)

    def emit(of, g, hh):
        at = 128 * (2 * (g - 1) + hh)
        first_col = (side if of == 0 else 1 - side) * 512 + at
        pltpu.make_async_copy(ost.at[of, :, pl.ds(at, 128)],
                              out.at[:, pl.ds(pl.multiple_of(first_col, 128), 128)], loc.at[3]).start()

    def weights(g, q, xi):
        def go():
            wait_w(g, q, xi)
            if 0 < q < 7 and xi != FAR:
                d = (q + 1) % 2
                src = slot(g, q, xi) if q < 5 else half(g, q, xi, d)
                on = q + 2
                push(src, slot(g, on, xi), rsem_of(g, on, xi), (up, down)[d], g)
            if xi == PAIR:
                cross(g, q)
        guarded(g, go)

    load_kv.wait()
    arrive(wbuf.at[0, pl.ds(0, 4)], loc.at[2])
    once = set()

    def first(name):
        new = name not in once
        once.add(name)
        return new

    for what, *a in ORDER:
        if what == "tables" and first("small"):
            for copy in small:
                copy.wait()
        if what in ("dots", "tokp", "tokp2") and first("tok"):
            load_tok.wait()
        if what == "near":
            start_near(*a)
        elif what == "pair":
            start_pair(*a)
        elif what == "tokp":
            tok_pair(0, *a)
        elif what == "tokp2":
            tok_pair(3, *a)
        elif what == "src":
            ring_start(*a)
        elif what == "w":
            weights(*a)
        elif what == "t":
            tok_arrived(*a)
        elif what == "sib":
            to_sibling(*a)
        elif what == "s":
            from_sibling(*a)
        elif what == "tables":
            tables(*a)
        elif what == "dots":
            dots(*a)
        elif what == "kv":
            kv_finish(*a)
            kv_send(*a)
        elif what == "kvin":
            for n in range(4):
                own[n] = query(0, 1 + n // 2, n % 2)
            kv_arrived()
        elif what == "q":
            send_queries(*a)
        elif what == "qin":
            n = 2 * (a[0] - 1) + a[1]
            arrive(qin.at[n], rq.at[n])
        elif what == "att":
            heads = (0, 1) if len(a) == 2 else a[2:]
            for hh in heads:
                attend(a[0], a[1], hh)
            for hh in heads:
                emit(a[0], a[1], hh)

    for g in (1, 2):
        arrive(group(g).at[pl.ds(0, 31)], send.at[g])
    arrive(tokb.at[1], send.at[S_TOK])
    arrive(qst, send.at[S_QUERY])

    @pl.when(worker)
    def _():
        arrive(kvbuf.at[pl.ds(0, 30)], send.at[S_KV])
        arrive(wbuf.at[0, pl.ds(0, 6)], send.at[S_KEYS])

    @pl.when(worker & (kv_to != y))
    def _():
        arrive(kvst.at[0], send.at[S_BEYOND])

    @pl.when(jnp.logical_not(worker))
    def _():
        arrive(kvbuf.at[0], send.at[S_HELP])

    arrive(ost, loc.at[3])


def shards(tokens, q_weight, kv_weight, q_gain, k_gain, doc_lengths):
    half = np.exp(np.arange(64) * (-2.0 * math.log(THETA) / HD)).astype(np.float32)
    freq = jnp.asarray(np.concatenate([half, half])[None, :])
    any_ = pl.BlockSpec(memory_space=pl.ANY)
    dma = pltpu.SemaphoreType.DMA
    operands = (tokens, q_weight, kv_weight, q_gain[None, :], k_gain[None, :], freq, doc_lengths.T)
    operands = [pltpu.with_memory_space_constraint(a, pltpu.HBM) for a in operands]
    return pl.pallas_call(
        kernel,
        out_shape=jax.ShapeDtypeStruct((ROWS, 1024), BF16),
        in_specs=[any_] * 7,
        out_specs=any_,
        scratch_shapes=[
            pltpu.VMEM((2, ROWS, FEAT), BF16),
            pltpu.VMEM((2, 32, 128, 256), BF16),
            pltpu.VMEM((32, 128, 128), BF16),
            pltpu.VMEM((2, 128, 256), BF16),
            pltpu.VMEM((2, 2, ROWS, 256), F32),
            pltpu.VMEM((2, ROWS, 128), F32),
            pltpu.VMEM((2, ROWS, 128), BF16),
            pltpu.VMEM((2, ROWS, 128), BF16),
            pltpu.VMEM((2, ROWS, HD), F32),
            pltpu.VMEM((2, ROWS, HD), F32),
            pltpu.VMEM((ROWS, ROWS), F32),
            pltpu.VMEM((2, ROWS, 512), BF16),
            pltpu.VMEM((4, ROWS, HD), BF16),
            pltpu.VMEM((4, ROWS, HD), BF16),
            pltpu.VMEM((4, ROWS, HD), BF16),
            pltpu.VMEM((1, HD), F32),
            pltpu.VMEM((1, HD), F32),
            pltpu.VMEM((1, HD), F32),
            pltpu.SMEM((16, 32), jnp.int32),
            dma((8,)),
            dma((3, 27)),
            dma((4, 8)),
            dma((1,)),
            dma((1,)),
            dma((4,)),
            dma((8,)),
        ],
        compiler_params=pltpu.CompilerParams(
            collective_id=0, has_side_effects=True, vmem_limit_bytes=24 * 2**20),
        cost_estimate=pl.CostEstimate(
            flops=6_000_000_000, bytes_accessed=12 * 2**20, transcendentals=2**21),
    )(*operands)


def solution(mesh):
    placed = (P("dp", None), P("dp", "head"), P("dp", "head"), P(), P(), P())
    return jax.shard_map(
        shards, mesh=mesh, in_specs=placed, out_specs=P("dp", "head"), check_vma=False
    )
```
